32 devices in a mesh: dp: 4 (over y, core), ctx: 8 (over z, x).
Axes of the slice: x: 2, y: 2, z: 4, core: 2. Of those that a mesh axis runs over, the one named last changes fastest.
Arguments:
- tokens_in: bfloat16 [4, 1024, 1024], P('dp', 'ctx'), may hold values from -6 to 6
- upstream: float32 [4, 1024, 1024], P('dp', 'ctx'), may hold values from -6 to 6
- query_weight: float32 [1024, 768], P(('dp', 'ctx')), may hold values from -0.1875 to 0.1875
- key_weight: float32 [1024, 768], P(('dp', 'ctx')), may hold values from -0.1875 to 0.1875
- value_weight: float32 [1024, 1536], P(('dp', 'ctx')), may hold values from -0.1875 to 0.1875
- gate_weight: float32 [1024, 1536], P(('dp', 'ctx')), may hold values from -0.1875 to 0.1875
- output_weight: float32 [1024, 1536], P(('dp', 'ctx')), may hold values from -0.15625 to 0.15625
- swiglu_gate: float32 [1024, 2816], P(('dp', 'ctx')), may hold values from -0.1875 to 0.1875
- swiglu_up: float32 [1024, 2816], P(('dp', 'ctx')), may hold values from -0.1875 to 0.1875
- swiglu_down: float32 [1024, 2816], P(('dp', 'ctx')), may hold values from -0.109375 to 0.109375
- query_moment: float32 [1024, 768], P(('dp', 'ctx'))
- key_moment: float32 [1024, 768], P(('dp', 'ctx'))
- value_moment: float32 [1024, 1536], P(('dp', 'ctx'))
- gate_moment: float32 [1024, 1536], P(('dp', 'ctx'))
- output_moment: float32 [1024, 1536], P(('dp', 'ctx'))
- swiglu_gate_moment: float32 [1024, 2816], P(('dp', 'ctx'))
- swiglu_up_moment: float32 [1024, 2816], P(('dp', 'ctx'))
- swiglu_down_moment: float32 [1024, 2816], P(('dp', 'ctx'))
- small_params: float32 [26892], replicated, may hold values from -8.5 to 1.5
- small_moment: float32 [26892], replicated, may hold values from -48 to 48
Outputs:
- block_out: float32 [4, 1024, 1024], P('dp', 'ctx')
- input_grad: float32 [4, 1024, 1024], P('dp', 'ctx')
- query_weight_grad: float32 [1024, 768], P(('dp', 'ctx'))
- key_weight_grad: float32 [1024, 768], P(('dp', 'ctx'))
- value_weight_grad: float32 [1024, 1536], P(('dp', 'ctx'))
- gate_weight_grad: float32 [1024, 1536], P(('dp', 'ctx'))
- output_weight_grad: float32 [1024, 1536], P(('dp', 'ctx'))
- swiglu_gate_grad: float32 [1024, 2816], P(('dp', 'ctx'))
- swiglu_up_grad: float32 [1024, 2816], P(('dp', 'ctx'))
- swiglu_down_grad: float32 [1024, 2816], P(('dp', 'ctx'))
- query_weight_new: float32 [1024, 768], P(('dp', 'ctx'))
- key_weight_new: float32 [1024, 768], P(('dp', 'ctx'))
- value_weight_new: float32 [1024, 1536], P(('dp', 'ctx'))
- gate_weight_new: float32 [1024, 1536], P(('dp', 'ctx'))
- output_weight_new: float32 [1024, 1536], P(('dp', 'ctx'))
- swiglu_gate_new: float32 [1024, 2816], P(('dp', 'ctx'))
- swiglu_up_new: float32 [1024, 2816], P(('dp', 'ctx'))
- swiglu_down_new: float32 [1024, 2816], P(('dp', 'ctx'))
- query_moment_new: float32 [1024, 768], P(('dp', 'ctx'))
- key_moment_new: float32 [1024, 768], P(('dp', 'ctx'))
- value_moment_new: float32 [1024, 1536], P(('dp', 'ctx'))
- gate_moment_new: float32 [1024, 1536], P(('dp', 'ctx'))
- output_moment_new: float32 [1024, 1536], P(('dp', 'ctx'))
- swiglu_gate_moment_new: float32 [1024, 2816], P(('dp', 'ctx'))
- swiglu_up_moment_new: float32 [1024, 2816], P(('dp', 'ctx'))
- swiglu_down_moment_new: float32 [1024, 2816], P(('dp', 'ctx'))
- small_grad: float32 [26892], replicated
- small_new: float32 [26892], replicated
- small_moment_new: float32 [26892], replicated
- moment_norms: float32 [8], replicated
The draws below stay inside these ranges and needn't reach their ends.
All inputs are finite; a program needn't handle non-finite values.
Results may differ from the reference program's by a relative error of at most 0.018.
Values may be sent and summed in bfloat16 or wider, within the bound.
No kernel may reach another device: no remote copies, remote signals or barrier semaphores. Data moves between devices by JAX's collectives and lax.ppermute only.
A program may use at most 320 MiB of HBM per device.

```python
import math
import jax
import jax.numpy as jnp
from jax import lax

D = 1024
H = 6
DK = 128
DV = 256
FF = 2816
CONV = 4
GROUP = 64
NS_STEPS = 3
SEQS = 4
LEN = 1024
KD = 768
VD = 1536
QKV = 3072
SMALL = 26892


def draw_small_params(key, part):
    pieces = jax.random.split(key, 5)
    gain_values = jnp.clip(1.0 + 0.15 * jax.random.normal(pieces[0], (2 * D + DV,), jnp.float32), 0.5, 1.5)
    decay_values = jax.random.uniform(pieces[2], (H,), jnp.float32, -8.0, -3.0)
    conv_values = jax.random.uniform(pieces[1], (CONV * QKV,), jnp.float32, -0.6, 0.6)
    bias_values = jax.random.uniform(pieces[3], (H,), jnp.float32, -1.0, 1.0)
    route_bound = (3.0 / D) ** 0.5
    route_values = jax.random.uniform(pieces[4], (D * 2 * H,), jnp.float32, -route_bound, route_bound)
    return jnp.concatenate([gain_values, conv_values, decay_values, bias_values, route_values])


def moment_rows(key, columns):
    position = jnp.arange(D, dtype=jnp.float32) / (D - 1)
    base = (SEQS * LEN) ** 0.5 / 8.0
    values = jnp.clip(jax.random.normal(key, (D, columns), jnp.float32), -3.0, 3.0)
    ramp = 1.0 + 2.0 * position
    return values * (base * ramp)[:, None]


def draw_query_moment(key, part):
    return moment_rows(jax.random.fold_in(key, 11), KD)


def draw_key_moment(key, part):
    return moment_rows(jax.random.fold_in(key, 12), KD)


def draw_value_moment(key, part):
    return moment_rows(jax.random.fold_in(key, 13), VD)


def draw_gate_moment(key, part):
    return moment_rows(jax.random.fold_in(key, 14), VD)


def draw_output_moment(key, part):
    return moment_rows(jax.random.fold_in(key, 15), VD)


def draw_swiglu_gate_moment(key, part):
    return moment_rows(jax.random.fold_in(key, 16), FF)


def draw_swiglu_up_moment(key, part):
    return moment_rows(jax.random.fold_in(key, 17), FF)


def draw_swiglu_down_moment(key, part):
    return moment_rows(jax.random.fold_in(key, 18), FF)


def strengthened(result, stream_key, source, target, parts, factor):
    def block_of(axis_at):
        return (jnp.arange(result.shape[axis_at]) // (result.shape[axis_at] // parts)).reshape((-1,) + (1,) * (result.ndim - 1 - axis_at))

    first = jax.random.permutation(stream_key, parts)[block_of(target)]
    other_side = (block_of(target) + parts // 2) % parts
    return jnp.where((block_of(source) == first) | (block_of(source) == other_side), factor * result, result)


def shard_levels(key, extent, shards, smallest, top_value):
    loudness = 1.0
    for dim, shards_of in shards:
        steps = jax.random.uniform(jax.random.fold_in(jax.random.fold_in(key, 6), dim), (shards_of,), jnp.float32, smallest / len(shards), top_value / len(shards))
        loudness = loudness * jnp.repeat(jnp.exp(steps), extent[dim] // shards_of).reshape((-1,) + (1,) * (len(extent) - 1 - dim))
    return loudness


def gaussian(stream_key, dims, spread, bound, cuts=(), kind=jnp.bfloat16):
    entries = spread * jax.random.normal(stream_key, dims, jnp.float32)
    if cuts:
        entries = entries * shard_levels(stream_key, dims, cuts, -0.22, 0.18)
    return jnp.clip(entries, -bound, bound).astype(kind)


def bell_draw_with(key, dims, width, most, cuts, heavy, kind=jnp.bfloat16):
    values = width * jax.random.normal(key, dims, jnp.float32)
    if cuts:
        values = values * shard_levels(key, dims, cuts, -0.22, 0.18)
    return jnp.clip(strengthened(values, jax.random.fold_in(key, 3), *heavy), -most, most).astype(kind)


def setup_inputs(seed: int = 0) -> dict:
    splits = jax.random.split(jax.random.key(seed), 21)
    return {
        "tokens_in": gaussian(splits[0], (SEQS, LEN, D), 1.0, 6.0, ((0, 4), (1, 8))),
        "upstream": bell_draw_with(splits[1], (SEQS, LEN, D), 1.0, 6.0, ((0, 4), (1, 8)), (1, 2, 8, 2.0), jnp.float32),
        "query_weight": gaussian(splits[2], (D, KD), D ** -0.5, 0.1875, ((0, 32),), jnp.float32),
        "key_weight": gaussian(splits[3], (D, KD), D ** -0.5, 0.1875, ((0, 32),), jnp.float32),
        "value_weight": gaussian(splits[4], (D, VD), D ** -0.5, 0.1875, ((0, 32),), jnp.float32),
        "gate_weight": gaussian(splits[5], (D, VD), D ** -0.5, 0.1875, ((0, 32),), jnp.float32),
        "output_weight": gaussian(splits[6], (D, VD), VD ** -0.5, 0.15625, ((0, 32),), jnp.float32),
        "swiglu_gate": gaussian(splits[7], (D, FF), D ** -0.5, 0.1875, ((0, 32),), jnp.float32),
        "swiglu_up": gaussian(splits[8], (D, FF), D ** -0.5, 0.1875, ((0, 32),), jnp.float32),
        "swiglu_down": gaussian(splits[9], (D, FF), FF ** -0.5, 0.109375, ((0, 32),), jnp.float32),
        "query_moment": draw_query_moment(jax.random.fold_in(splits[20], 71), 0),
        "key_moment": draw_key_moment(jax.random.fold_in(splits[20], 71), 0),
        "value_moment": draw_value_moment(jax.random.fold_in(splits[20], 71), 0),
        "gate_moment": draw_gate_moment(jax.random.fold_in(splits[20], 71), 0),
        "output_moment": draw_output_moment(jax.random.fold_in(splits[20], 71), 0),
        "swiglu_gate_moment": draw_swiglu_gate_moment(jax.random.fold_in(splits[20], 71), 0),
        "swiglu_up_moment": draw_swiglu_up_moment(jax.random.fold_in(splits[20], 71), 0),
        "swiglu_down_moment": draw_swiglu_down_moment(jax.random.fold_in(splits[20], 71), 0),
        "small_params": draw_small_params(jax.random.fold_in(splits[20], 71), 0),
        "small_moment": gaussian(splits[19], (SMALL,), (0.125 * (SEQS * LEN) ** 0.5), 48.0, (), jnp.float32),
    }


highest_precision = lax.Precision.HIGHEST
eps_norm = 1e-05
eps_unit = 1e-06
eps_muon = 1e-07
moment_rate = 0.95
matrix_rate = 0.3
small_rate = 0.002
poly_one = 3.4445
poly_two = -4.775
poly_three = 2.0315

def matmul(left, right):
    return jnp.dot(left.astype(jnp.float32), right.astype(jnp.float32), preferred_element_type=jnp.float32)

def times_transposed(left, right):
    return lax.dot_general(left.astype(jnp.float32), right.astype(jnp.float32), (((1,), (1,)), ((), ())), preferred_element_type=jnp.float32)

def transposed_times(left, right):
    return lax.dot_general(left.astype(jnp.float32), right.astype(jnp.float32), (((0,), (0,)), ((), ())), preferred_element_type=jnp.float32)

def root_norm(values, gain):
    return values * lax.rsqrt(lax.optimization_barrier(jnp.mean(values * values, axis=-1, keepdims=True)) + eps_norm) * gain

def unit_rows(values):
    return values * lax.rsqrt(lax.optimization_barrier(jnp.sum(values * values, axis=-1, keepdims=True)) + eps_unit)

def unpack_small(packed):
    lengths = [D, D, DV, CONV * QKV, H, H, D * 2 * H]
    pieces = []
    offset = 0
    for length in lengths:
        pieces.append(packed[offset:offset + length])
        offset = offset + length
    return (pieces[0], pieces[1], pieces[2], pieces[3].reshape(CONV, QKV), pieces[4], pieces[5], pieces[6].reshape(D, 2 * H))

def pack_small(members):
    return jnp.concatenate([member.reshape(-1) for member in members])

def conv_silu(extended, conv_taps):
    kernel_size = conv_taps.shape[0]
    rows_out = extended.shape[0] - kernel_size + 1
    summed = jnp.zeros((rows_out, extended.shape[1]), jnp.float32)
    for offset in range(kernel_size):
        summed = summed + conv_taps[offset] * extended[offset:offset + rows_out]
    return jax.nn.silu(summed)

def mixer_inputs(extended, route_pre, conv_taps, decay_log, decay_bias):
    conv_out = conv_silu(extended, conv_taps)
    rows_now = conv_out.shape[0]
    queries = unit_rows(conv_out[:, :KD].reshape(rows_now, H, DK)) * DK ** (-0.5)
    keys_all = unit_rows(conv_out[:, KD:2 * KD].reshape(rows_now, H, DK))
    values = conv_out[:, 2 * KD:].reshape(rows_now, H, DV)
    betas = jax.nn.sigmoid(route_pre[:, :H])
    log_decay = -jnp.exp(decay_log) * jax.nn.softplus(route_pre[:, H:] + decay_bias)
    return (queries, keys_all, values, betas, log_decay)

def solve_unit(matrix, target):
    return jax.scipy.linalg.solve_triangular(matrix, target, lower=True, unit_diagonal=True)

def group_terms(queries, keys_all, values, betas, log_decay):
    head_query = jnp.transpose(queries, (1, 0, 2))
    key_head = jnp.transpose(keys_all, (1, 0, 2))
    value_head = jnp.transpose(values, (1, 0, 2))
    beta_head = jnp.transpose(betas)
    cumulative = jnp.cumsum(jnp.transpose(log_decay), axis=1)
    positions = jnp.arange(cumulative.shape[1])
    inclusive = positions[:, None] >= positions[None, :]
    strictly = positions[:, None] > positions[None, :]
    differ = cumulative[:, :, None] - cumulative[:, None, :]
    within = jnp.where(inclusive, jnp.exp(jnp.where(inclusive, differ, 0.0)), 0.0)
    key_key = jnp.einsum('htd,hsd->hts', key_head, key_head, precision=highest_precision)
    lower_part = jnp.where(strictly, beta_head[:, :, None] * within * key_key, 0.0)
    growth_factor = jnp.exp(cumulative)
    system = jnp.eye(cumulative.shape[1], dtype=jnp.float32)[None] + lower_part
    right_keys = (beta_head * growth_factor)[:, :, None] * key_head
    right_values = beta_head[:, :, None] * value_head
    triangular_keys = jax.vmap(solve_unit)(system, right_keys)
    triangular_values = jax.vmap(solve_unit)(system, right_values)
    attend = within * jnp.einsum('htd,hsd->hts', head_query, key_head, precision=highest_precision)
    tail_decay = jnp.exp(cumulative[:, -1:] - cumulative)
    beta_scaled_keys = key_head * tail_decay[:, :, None]
    identity = jnp.eye(DK, dtype=jnp.float32)
    transition = growth_factor[:, -1][:, None, None] * identity[None] - jnp.einsum('hck,hcj->hkj', beta_scaled_keys, triangular_keys, precision=highest_precision)
    shifted_state = jnp.einsum('aom,aos->ams', beta_scaled_keys, triangular_values, precision=highest_precision)
    return (head_query, growth_factor, attend, triangular_keys, triangular_values, transition, shifted_state)

def group_all(queries, keys_all, values, betas, log_decay):
    blocks = queries.shape[0] // GROUP

    def split_blocks(member):
        return member.reshape((blocks, GROUP) + member.shape[1:])
    return jax.vmap(group_terms)(split_blocks(queries), split_blocks(keys_all), split_blocks(values), split_blocks(betas), split_blocks(log_decay))

def apply_groups(terms, state_in):

    def advance(carry_state, group_term):
        head_query, growth_factor, attend, triangular_keys, triangular_values, transition, shifted_state = group_term
        pseudo_value = triangular_values - jnp.einsum('uqb,ubi->uqi', triangular_keys, carry_state, precision=highest_precision)
        output_rows = growth_factor[:, :, None] * jnp.einsum('uqb,ubi->uqi', head_query, carry_state, precision=highest_precision)
        output_rows = output_rows + jnp.einsum('hts,hsv->htv', attend, pseudo_value, precision=highest_precision)
        following = jnp.einsum('hij,hjv->hiv', transition, carry_state, precision=highest_precision) + shifted_state
        return (following, output_rows)
    final_state, stacked = lax.scan(advance, state_in, terms)
    output_rows = jnp.transpose(stacked, (0, 2, 1, 3)).reshape(-1, H, DV)
    return (output_rows, final_state)

def gate_outputs(output_rows, gate_pre, head_gain):
    normed = output_rows * lax.rsqrt(lax.optimization_barrier(jnp.mean(output_rows * output_rows, axis=-1, keepdims=True)) + eps_norm) * head_gain
    gated = normed * jax.nn.silu(gate_pre.reshape(output_rows.shape))
    return gated.reshape(output_rows.shape[0], VD)

def mixer_core(extended, route_pre, gate_pre, conv_taps, decay_log, decay_bias, head_gain, state_in):
    inputs = mixer_inputs(extended, route_pre, conv_taps, decay_log, decay_bias)
    terms = group_all(*inputs)
    output_rows, final_state = apply_groups(terms, state_in)
    return (gate_outputs(output_rows, gate_pre, head_gain), final_state)

def sequence_pass(weights_low, small_parts, tokens_seq, upstream_seq):
    query_low, key_low, value_low, gate_low, output_low, swiglu_gate_low, swiglu_up_low, swiglu_down_low = weights_low
    gain_one, gain_two, head_gain, conv_taps, decay_log, decay_bias, route_weight = small_parts
    route_low = route_weight.astype(jnp.bfloat16)
    inputs_full = tokens_seq.astype(jnp.float32)
    normed_one, norm_one_back = jax.vjp(root_norm, inputs_full, gain_one)
    normed_one_low = normed_one.astype(jnp.bfloat16)
    pre_proj = jnp.concatenate([matmul(normed_one_low, query_low), matmul(normed_one_low, key_low), matmul(normed_one_low, value_low)], axis=1)
    gate_pre = matmul(normed_one_low, gate_low)
    route_pre = matmul(normed_one_low, route_low)
    extended = jnp.concatenate([jnp.zeros((CONV - 1, QKV), jnp.float32), pre_proj], axis=0)
    state_zero = jnp.zeros((H, DK, DV), jnp.float32)

    def mixer_local(extended, route_pre, gate_pre, conv_taps, decay_log, decay_bias, head_gain):
        return mixer_core(extended, route_pre, gate_pre, conv_taps, decay_log, decay_bias, head_gain, state_zero)[0]
    mixed, mixer_back = jax.vjp(mixer_local, extended, route_pre, gate_pre, conv_taps, decay_log, decay_bias, head_gain)
    mixed_low = mixed.astype(jnp.bfloat16)
    residual_one = inputs_full + times_transposed(mixed_low, output_low)
    normed_two, norm_two_back = jax.vjp(root_norm, residual_one, gain_two)
    normed_two_low = normed_two.astype(jnp.bfloat16)
    gate_act = matmul(normed_two_low, swiglu_gate_low)
    up_act = matmul(normed_two_low, swiglu_up_low)
    middle = (jax.nn.silu(gate_act) * up_act).astype(jnp.bfloat16)
    block_out = residual_one + times_transposed(middle, swiglu_down_low)
    upstream_low = upstream_seq.astype(jnp.bfloat16)
    grad_middle = matmul(upstream_low, swiglu_down_low)
    swiglu_down_grad = transposed_times(upstream_low, middle)
    sigma = jax.nn.sigmoid(gate_act)
    grad_gate = (grad_middle * up_act * sigma * (1.0 + gate_act * (1.0 - sigma))).astype(jnp.bfloat16)
    grad_up = (grad_middle * gate_act * sigma).astype(jnp.bfloat16)
    swiglu_gate_grad = transposed_times(normed_two_low, grad_gate)
    swiglu_up_grad = transposed_times(normed_two_low, grad_up)
    grad_normed_two = times_transposed(grad_gate, swiglu_gate_low) + times_transposed(grad_up, swiglu_up_low)
    grad_residual_norm, grad_gain_two = norm_two_back(grad_normed_two)
    grad_residual = upstream_seq + grad_residual_norm
    grad_residual_low = grad_residual.astype(jnp.bfloat16)
    grad_mixed = matmul(grad_residual_low, output_low)
    output_weight_grad = transposed_times(grad_residual_low, mixed_low)
    grad_extended, grad_route_pre, grad_gate_pre, grad_conv_taps, grad_decay_log, grad_decay_bias, grad_head_gain = mixer_back(grad_mixed)
    grad_pre_low = grad_extended[CONV - 1:].astype(jnp.bfloat16)
    grad_gate_pre_low = grad_gate_pre.astype(jnp.bfloat16)
    grad_route_low = grad_route_pre.astype(jnp.bfloat16)
    query_weight_grad = transposed_times(normed_one_low, grad_pre_low[:, :KD])
    key_weight_grad = transposed_times(normed_one_low, grad_pre_low[:, KD:2 * KD])
    value_weight_grad = transposed_times(normed_one_low, grad_pre_low[:, 2 * KD:])
    gate_weight_grad = transposed_times(normed_one_low, grad_gate_pre_low)
    route_weight_grad = transposed_times(normed_one_low, grad_route_low)
    grad_normed_one = times_transposed(grad_pre_low[:, :KD], query_low) + times_transposed(grad_pre_low[:, KD:2 * KD], key_low)
    grad_normed_one = grad_normed_one + times_transposed(grad_pre_low[:, 2 * KD:], value_low)
    grad_normed_one = grad_normed_one + times_transposed(grad_gate_pre_low, gate_low) + times_transposed(grad_route_low, route_low)
    grad_inputs, grad_gain_one = norm_one_back(grad_normed_one)
    input_grad = grad_residual + grad_inputs
    small_grad = pack_small((grad_gain_one, grad_gain_two, grad_head_gain, grad_conv_taps, grad_decay_log, grad_decay_bias, route_weight_grad))
    matrix_grads = (query_weight_grad, key_weight_grad, value_weight_grad, gate_weight_grad, output_weight_grad, swiglu_gate_grad, swiglu_up_grad, swiglu_down_grad)
    return (block_out, input_grad, matrix_grads, small_grad)

def newton_schulz(start_low):
    iterate = start_low
    for step_index in range(NS_STEPS):
        gram_low = lax.optimization_barrier(times_transposed(iterate, iterate).astype(jnp.bfloat16))
        squared = matmul(gram_low, gram_low)
        polynomial = (poly_two * gram_low.astype(jnp.float32) + poly_three * squared).astype(jnp.bfloat16)
        iterate = lax.optimization_barrier((poly_one * iterate.astype(jnp.float32) + matmul(polynomial, iterate)).astype(jnp.bfloat16))
    return iterate

def reference(tokens_in, upstream, query_weight, key_weight, value_weight, gate_weight, output_weight, swiglu_gate, swiglu_up, swiglu_down, query_moment, key_moment, value_moment, gate_moment, output_moment, swiglu_gate_moment, swiglu_up_moment, swiglu_down_moment, small_params, small_moment):
    weights_in = (query_weight, key_weight, value_weight, gate_weight, output_weight, swiglu_gate, swiglu_up, swiglu_down)
    moments_in = (query_moment, key_moment, value_moment, gate_moment, output_moment, swiglu_gate_moment, swiglu_up_moment, swiglu_down_moment)
    weights_low = tuple((member.astype(jnp.bfloat16) for member in weights_in))
    small_parts = unpack_small(small_params)

    def one_sequence(carry_state, inputs_pair):
        tokens_seq, upstream_seq = inputs_pair
        block_out, input_grad, matrix_grads, small_grad = sequence_pass(weights_low, small_parts, tokens_seq, upstream_seq)
        carry_state = jax.tree.map(jnp.add, carry_state, (matrix_grads, small_grad))
        return (carry_state, (block_out, input_grad))
    zero_grads = (tuple((jnp.zeros(member.shape, jnp.float32) for member in weights_in)), jnp.zeros(small_params.shape, jnp.float32))
    summed, output_rows = lax.scan(one_sequence, zero_grads, (tokens_in, upstream))
    matrix_grads, small_grad = summed
    block_out, input_grad = output_rows
    weights_new = []
    moments_new = []
    norm_list = []
    for index in range(8):
        moment_new = moment_rate * moments_in[index] + matrix_grads[index]
        norm_value = jnp.sqrt(jnp.sum(moment_new * moment_new))
        start_low = lax.optimization_barrier((moment_new / (norm_value + eps_muon)).astype(jnp.bfloat16))
        ortho = newton_schulz(start_low)
        factor = matrix_rate * math.sqrt(max(1.0, weights_in[index].shape[1] / D))
        weights_new.append(weights_in[index] - factor * ortho.astype(jnp.float32))
        moments_new.append(moment_new)
        norm_list.append(norm_value)
    moment_norms = jnp.stack(norm_list)
    small_moment_new = moment_rate * small_moment + small_grad
    small_new = small_params - small_rate * small_moment_new
    return (block_out, input_grad, matrix_grads[0], matrix_grads[1], matrix_grads[2], matrix_grads[3], matrix_grads[4], matrix_grads[5], matrix_grads[6], matrix_grads[7], weights_new[0], weights_new[1], weights_new[2], weights_new[3], weights_new[4], weights_new[5], weights_new[6], weights_new[7], moments_new[0], moments_new[1], moments_new[2], moments_new[3], moments_new[4], moments_new[5], moments_new[6], moments_new[7], small_grad, small_new, small_moment_new, moment_norms)
```

```python
import math

import jax
import jax.numpy as jnp
from jax import lax
from jax.experimental import pallas as pl
from jax.sharding import PartitionSpec as P

D = 1024
H = 6
DK = 128
DV = 256
CONV = 4
GROUP = 64
NS_STEPS = 3
KD = 768
VD = 1536
QKV = 3072
FF = 2816
BOTH_AXES = ("dp", "ctx")


highest_precision = lax.Precision.HIGHEST
eps_norm = 1e-05
eps_unit = 1e-06
eps_muon = 1e-07
moment_rate = 0.95
matrix_rate = 0.3
small_rate = 0.002
poly_one = 3.4445
poly_two = -4.775
poly_three = 2.0315


def passed_along(value, axis, steps):
    count = lax.axis_size(axis)
    first, last = (max(0, -steps), min(count, count - steps))
    return lax.ppermute(value, axis, [(source, source + steps) for source in range(first, last)])


def shortened(array):
    return jax.tree.map(lambda a: a.astype(jnp.bfloat16) if a.dtype == jnp.float32 else a, array)


def matmul(left, right):
    return jnp.dot(left, right, preferred_element_type=jnp.float32)


def times_transposed(left, right):
    return lax.dot_general(
        left, right, (((1,), (1,)), ((), ())), preferred_element_type=jnp.float32
    )


def transposed_times(left, right):
    return lax.dot_general(
        left, right, (((0,), (0,)), ((), ())), preferred_element_type=jnp.float32
    )


def root_norm(values, gain):
    return values * lax.rsqrt(jnp.mean(values * values, axis=-1, keepdims=True) + eps_norm) * gain


def unit_rows(values):
    return values * lax.rsqrt(jnp.sum(values * values, axis=-1, keepdims=True) + eps_unit)


def unpack_small(packed):
    lengths = [D, D, DV, CONV * QKV, H, H, D * 2 * H]
    pieces = []
    offset = 0
    for length in lengths:
        pieces.append(packed[offset : offset + length])
        offset = offset + length
    return (
        pieces[0],
        pieces[1],
        pieces[2],
        pieces[3].reshape(CONV, QKV),
        pieces[4],
        pieces[5],
        pieces[6].reshape(D, 2 * H),
    )


def pack_small(members):
    return jnp.concatenate([member.reshape(-1) for member in members])


def conv_silu(extended, conv_taps):
    kernel_size = conv_taps.shape[0]
    rows_out = extended.shape[0] - kernel_size + 1
    summed = jnp.zeros((rows_out, extended.shape[1]), jnp.float32)
    for offset in range(kernel_size):
        summed = summed + conv_taps[offset] * extended[offset : offset + rows_out]
    return jax.nn.silu(summed)


def raw_dot(left, right, left_dim, right_dim):
    return lax.dot_general(
        left,
        right,
        (((left_dim,), (right_dim,)), ((), ())),
        precision=highest_precision,
        preferred_element_type=jnp.float32,
    )


@jax.custom_vjp
def mm(left, right):
    return raw_dot(left, right, 1, 0)


@jax.custom_vjp
def mm_nt(left, right):
    return raw_dot(left, right, 1, 1)


@jax.custom_vjp
def mm_tn(left, right):
    return raw_dot(left, right, 0, 0)


def keep_operands(function):
    return lambda left, right: (function(left, right), (left, right))


mm.defvjp(
    keep_operands(mm),
    lambda kept, grad: (raw_dot(grad, kept[1], 1, 1), raw_dot(kept[0], grad, 0, 0)),
)
mm_nt.defvjp(
    keep_operands(mm_nt),
    lambda kept, grad: (raw_dot(grad, kept[1], 1, 0), raw_dot(grad, kept[0], 0, 0)),
)
mm_tn.defvjp(
    keep_operands(mm_tn),
    lambda kept, grad: (raw_dot(kept[1], grad, 1, 1), raw_dot(kept[0], grad, 1, 0)),
)


def position_pair(rows, columns):
    return (
        lax.broadcasted_iota(jnp.int32, (rows, columns), 0),
        lax.broadcasted_iota(jnp.int32, (rows, columns), 1),
    )


def widened(member, columns):
    copies = columns // member.shape[1]
    return member if copies == 1 else jnp.concatenate([member] * copies, axis=1)


def head_masks(rows):
    at, source = position_pair(rows, rows)
    same = at // GROUP == source // GROUP
    return same, same & (at >= source), same & (at > source)


def unit_inverse(lower):
    rows = lower.shape[0]
    at, source = position_pair(rows, rows)

    def step_part(block):
        inside = (at // (2 * block) == source // (2 * block)) & (at // block != source // block)
        return jnp.where(inside, lower, 0.0)

    result = jnp.where(at == source, 1.0, 0.0) - step_part(1)
    block = 2
    while block < GROUP:
        result = result - raw_dot(result, raw_dot(step_part(block), result, 1, 0), 1, 0)
        block = 2 * block
    return result


@jax.custom_vjp
def solved(lower, target, inverse):
    return raw_dot(inverse, target, 1, 0)


def solved_forward(lower, target, inverse):
    result = raw_dot(inverse, target, 1, 0)
    return (result, (inverse, result))


def solved_backward(kept, grad):
    inverse, result = kept
    target_grad = raw_dot(inverse, grad, 0, 0)
    return (-raw_dot(target_grad, result, 1, 1), target_grad, jnp.zeros_like(inverse))


solved.defvjp(solved_forward, solved_backward)


def decay_parts(log_wide):
    rows = log_wide.shape[0]
    at, source = position_pair(rows, rows)
    same, inclusive, strictly = head_masks(rows)
    growth = jnp.exp(mm(inclusive.astype(jnp.float32), log_wide))
    tail = jnp.exp(mm((same & ~inclusive).astype(jnp.float32), log_wide))
    differ = mm(inclusive.astype(jnp.float32), jnp.where(at > source, log_wide, 0.0))
    within = jnp.where(inclusive, jnp.exp(jnp.where(inclusive, differ, 0.0)), 0.0)
    return growth, tail, within


def group_decay(log_wide, group):
    rows = log_wide.shape[0]
    source = lax.broadcasted_iota(jnp.int32, (DK, rows), 1)
    return jnp.exp(mm((source // GROUP == group).astype(jnp.float32), log_wide))


def in_group(member, group):
    row = lax.broadcasted_iota(jnp.int32, member.shape, 0)
    return jnp.where(row // GROUP == group, member, 0.0)


def lower_system(keys, beta_wide, within):
    unused_same, unused_inclusive, strictly = head_masks(keys.shape[0])
    return jnp.where(strictly, beta_wide * within * mm_nt(keys, keys), 0.0)


def solve_targets(keys, values, beta_wide, growth):
    return jnp.concatenate(
        [beta_wide * growth * keys, widened(beta_wide, DV) * values], axis=1
    )


def head_terms(queries, keys, values, beta_wide, log_wide):
    growth, tail, within = decay_parts(log_wide)
    lower = lower_system(keys, beta_wide, within)
    inverse = unit_inverse(lower)
    both = raw_dot(inverse, solve_targets(keys, values, beta_wide, growth), 1, 0)
    solved_keys = both[:, :DK]
    at, source = position_pair(DK, DK + DV)
    state = jnp.where(at == source, 1.0, 0.0)
    offset_rows = jnp.where(
        lax.broadcasted_iota(jnp.int32, both.shape, 1) >= DK, both, 0.0
    )
    decayed_keys = keys * tail
    for group in range(keys.shape[0] // GROUP):
        pseudo = offset_rows - mm(solved_keys, state)
        state = widened(group_decay(log_wide, group), DK + DV) * state + mm_tn(
            in_group(decayed_keys, group), pseudo
        )
    return inverse, both, state


def head_outputs(queries, keys, log_wide, both, gate_pre, head_gain, state):
    growth, tail, within = decay_parts(log_wide)
    attend = within * mm_nt(queries, keys)
    decayed_keys = keys * tail
    solved_keys, solved_values = both[:, :DK], both[:, DK:]
    stacked = jnp.concatenate([queries, solved_keys], axis=0)
    rows = queries.shape[0]
    read = 0.0
    for group in range(rows // GROUP):
        now = mm(stacked, state)
        pseudo_now = solved_values - now[rows:]
        read = read + jnp.concatenate(
            [in_group(now[:rows], group), in_group(now[rows:], group)], axis=0
        )
        state = widened(group_decay(log_wide, group), DV) * state + mm_tn(
            in_group(decayed_keys, group), pseudo_now
        )
    output_rows = widened(growth, DV) * read[:rows] + mm(attend, solved_values - read[rows:])
    normed = (
        output_rows
        * lax.rsqrt(jnp.mean(output_rows * output_rows, axis=-1, keepdims=True) + eps_norm)
        * head_gain
    )
    return normed * (gate_pre * jax.nn.sigmoid(gate_pre)), state


def head_whole(inverse, state, queries, keys, values, beta_wide, log_wide, gate_pre, head_gain):
    growth, tail, within = decay_parts(log_wide)
    lower = lower_system(keys, beta_wide, within)
    both = solved(lower, solve_targets(keys, values, beta_wide, growth), inverse)
    return head_outputs(queries, keys, log_wide, both, gate_pre, head_gain, state)


def unit_rows_scaled(values, factor):
    return values * lax.rsqrt(jnp.sum(values * values, axis=-1, keepdims=True) + eps_unit) * factor


def rate_columns(rates, head):
    lane = lax.broadcasted_iota(jnp.int32, rates.shape, 1)
    beta = jnp.sum(jnp.where(lane == head, rates, 0.0), axis=1, keepdims=True)
    log_decay = jnp.sum(jnp.where(lane == head + H, rates, 0.0), axis=1, keepdims=True)
    wide = (rates.shape[0], DK)
    return jnp.broadcast_to(beta, wide), jnp.broadcast_to(log_decay, wide)


def head_inputs(query_conv, key_conv, rates, head):
    queries = unit_rows_scaled(query_conv, DK ** (-0.5))
    keys = unit_rows_scaled(key_conv, 1.0)
    beta_wide, log_wide = rate_columns(rates, head)
    return queries, keys, beta_wide, log_wide


def terms_kernel(query_ref, key_ref, value_ref, rates_ref, inverse_ref, both_ref, map_ref):
    queries, keys, beta_wide, log_wide = head_inputs(
        query_ref[...], key_ref[...], rates_ref[...], pl.program_id(0)
    )
    inverse, both, state = head_terms(queries, keys, value_ref[...], beta_wide, log_wide)
    inverse_ref[...] = inverse
    both_ref[...] = both
    map_ref[0] = state


def outputs_kernel(
    query_ref, key_ref, rates_ref, both_ref, gate_ref, gain_ref, state_ref, mixed_ref
):
    queries, keys, beta_wide, log_wide = head_inputs(
        query_ref[...], key_ref[...], rates_ref[...], pl.program_id(0)
    )
    mixed, unused = head_outputs(
        queries, keys, log_wide, both_ref[...], gate_ref[...], gain_ref[...], state_ref[0]
    )
    mixed_ref[...] = mixed.astype(mixed_ref.dtype)


def state_kernel(
    query_ref, key_ref, rates_ref, both_ref, gate_ref, gain_ref, state_ref, grad_ref, out_ref
):
    queries, keys, beta_wide, log_wide = head_inputs(
        query_ref[...], key_ref[...], rates_ref[...], pl.program_id(0)
    )

    def from_state(state):
        return head_outputs(
            queries, keys, log_wide, both_ref[...], gate_ref[...], gain_ref[...], state
        )[0]

    unused, back = jax.vjp(from_state, state_ref[0])
    out_ref[0] = back(grad_ref[...])[0]


def backward_kernel(
    inverse_ref,
    state_ref,
    query_ref,
    key_ref,
    value_ref,
    rates_ref,
    gate_ref,
    gain_ref,
    grad_ref,
    state_grad_ref,
    query_out,
    key_out,
    value_out,
    rates_out,
    gate_out,
    gain_out,
):
    inverse, state = inverse_ref[...], state_ref[0]
    head = pl.program_id(0)

    def whole(query_conv, key_conv, values, rates, gate_pre, gain):
        queries, keys, beta_wide, log_wide = head_inputs(query_conv, key_conv, rates, head)
        return head_whole(
            inverse, state, queries, keys, values, beta_wide, log_wide, gate_pre, gain
        )

    unused, back = jax.vjp(
        whole,
        query_ref[...],
        key_ref[...],
        value_ref[...],
        rates_ref[...],
        gate_ref[...],
        gain_ref[...],
    )
    grads = back((grad_ref[...], state_grad_ref[0]))
    query_out[...] = grads[0]
    key_out[...] = grads[1]
    value_out[...] = grads[2]
    gate_out[...] = grads[4].astype(gate_out.dtype)
    gain_out[0] = grads[5]

    @pl.when(head == 0)
    def first_head():
        rates_out[...] = grads[3]

    @pl.when(head > 0)
    def later_head():
        rates_out[...] = rates_out[...] + grads[3]


def columns_of(rows, width, first=0):
    return pl.BlockSpec((rows, width), lambda head: (0, head + first))


def matrix_of(rows, width):
    return pl.BlockSpec((1, rows, width), lambda head: (head, 0, 0))


def fixed_block(rows, width):
    return pl.BlockSpec((rows, width), lambda head: (0, 0))


def per_head(kernel, in_specs, out_specs, out_shapes):
    return pl.pallas_call(
        kernel, grid=(H,), in_specs=in_specs, out_specs=out_specs, out_shape=out_shapes
    )


def shape_of(*dims, kind=jnp.float32):
    return jax.ShapeDtypeStruct(dims, kind)


def run_terms(conv_out, rates):
    rows = conv_out.shape[0]
    return per_head(
        terms_kernel,
        [
            columns_of(rows, DK),
            columns_of(rows, DK, H),
            columns_of(rows, DV, 2 * KD // DV),
            fixed_block(rows, 2 * H),
        ],
        [columns_of(rows, rows), columns_of(rows, DK + DV), matrix_of(DK, DK + DV)],
        [
            shape_of(rows, H * rows),
            shape_of(rows, H * (DK + DV)),
            shape_of(H, DK, DK + DV),
        ],
    )(conv_out, conv_out, conv_out, rates)


def output_specs(rows):
    return [
        columns_of(rows, DK),
        columns_of(rows, DK, H),
        fixed_block(rows, 2 * H),
        columns_of(rows, DK + DV),
        columns_of(rows, DV, QKV // DV),
        fixed_block(1, DV),
        matrix_of(DK, DV),
    ]


def run_outputs(conv_out, rates, both, projected, gain_row, state):
    rows = conv_out.shape[0]
    return per_head(
        outputs_kernel,
        output_specs(rows),
        columns_of(rows, DV),
        shape_of(rows, H * DV, kind=jnp.bfloat16),
    )(conv_out, conv_out, rates, both, projected, gain_row, state)


def run_state(conv_out, rates, both, projected, gain_row, state, grad):
    rows = conv_out.shape[0]
    return per_head(
        state_kernel,
        output_specs(rows) + [columns_of(rows, DV)],
        matrix_of(DK, DV),
        shape_of(H, DK, DV),
    )(conv_out, conv_out, rates, both, projected, gain_row, state, grad)


def run_backward(inverse, state, conv_out, rates, projected, gain_row, grad, state_grad):
    rows = conv_out.shape[0]
    narrow, wide = columns_of(rows, DK), columns_of(rows, DV)
    return per_head(
        backward_kernel,
        [
            columns_of(rows, rows),
            matrix_of(DK, DV),
            narrow,
            columns_of(rows, DK, H),
            columns_of(rows, DV, 2 * KD // DV),
            fixed_block(rows, 2 * H),
            columns_of(rows, DV, QKV // DV),
            fixed_block(1, DV),
            wide,
            matrix_of(DK, DV),
        ],
        [narrow, narrow, wide, fixed_block(rows, 2 * H), wide, matrix_of(1, DV)],
        [
            shape_of(rows, H * DK),
            shape_of(rows, H * DK),
            shape_of(rows, H * DV),
            shape_of(rows, 2 * H),
            shape_of(rows, H * DV, kind=jnp.bfloat16),
            shape_of(H, 1, DV),
        ],
    )(
        inverse,
        state,
        conv_out,
        conv_out,
        conv_out,
        rates,
        projected,
        gain_row,
        grad,
        state_grad,
    )


def rate_parts(route_pre, decay_log, decay_bias):
    betas = jax.nn.sigmoid(route_pre[:, :H])
    log_decay = -jnp.exp(decay_log) * jax.nn.softplus(route_pre[:, H:] + decay_bias)
    return jnp.concatenate([betas, log_decay], axis=1)


def map_times(left, right):
    return jnp.einsum("hij,hjv->hiv", left, right, precision=highest_precision)


def sent_low(value, steps):
    return passed_along(value.astype(jnp.bfloat16), "ctx", steps).astype(jnp.float32)


def window_maps(trans, direction):
    count = lax.axis_size("ctx")
    levels = [trans]
    window = 1
    while 2 * window < count:
        levels.append(map_times(levels[-1], sent_low(levels[-1], direction * window)))
        window = 2 * window
    return levels, sent_low(levels[-1], direction)


def carried_state(levels, near_trans, offset, direction):
    window = 1
    for trans in levels[:-1]:
        offset = offset + map_times(trans, sent_low(offset, direction * window))
        window = 2 * window
    near = sent_low(offset, direction)
    far = sent_low(offset, direction * (window + 1))
    return near + map_times(near_trans, far)


def swap_columns(rows, count):
    split = rows.reshape(rows.shape[0], count, rows.shape[1] // count)
    return jnp.transpose(split, (1, 0, 2))


def summed_rows(terms, columns):
    dp_count, ctx_count = lax.axis_size("dp"), lax.axis_size("ctx")
    parts = lax.all_to_all(
        terms.reshape(dp_count, D // dp_count, columns), "dp", split_axis=0, concat_axis=0, tiled=True
    )
    block = jnp.sum(parts.astype(jnp.float32), axis=0).astype(jnp.bfloat16)
    rows = D // (dp_count * ctx_count)
    return lax.all_to_all(
        block.reshape(ctx_count, rows, columns), "ctx", split_axis=0, concat_axis=0, tiled=True
    )


def joined_columns(blocks):
    count, rows, columns = blocks.shape
    return jnp.transpose(blocks, (1, 0, 2)).reshape(rows, count * columns).astype(jnp.float32)


def summed_everywhere(vector):
    count = lax.axis_size("dp") * lax.axis_size("ctx")
    chunk = -(-vector.shape[0] // (count * 128)) * 128
    padded = jnp.pad(vector, (0, count * chunk - vector.shape[0])).reshape(count, chunk)
    parts = lax.all_to_all(padded, BOTH_AXES, split_axis=0, concat_axis=0, tiled=True)
    total = jnp.broadcast_to(jnp.sum(parts, axis=0)[None], (count, chunk))
    whole = lax.all_to_all(total, BOTH_AXES, split_axis=0, concat_axis=0, tiled=True)
    return whole.reshape(-1)[: vector.shape[0]]


def square_times(left, right):
    return jnp.dot(left, right, preferred_element_type=jnp.float32)


def orthogonal_rows(raw_rows):
    low = jnp.bfloat16
    raw = lax.all_gather(raw_rows, "dp", axis=0, tiled=True)
    gram_raw = times_transposed(raw, raw)
    norm = jnp.sqrt(jnp.trace(gram_raw))
    scale = 1.0 / (norm + eps_muon)
    gram = gram_raw * (scale * scale)
    factors = []
    for step in range(NS_STEPS):
        gram_low = gram.astype(low)
        factor = (poly_two * gram + poly_three * square_times(gram_low, gram_low)).astype(low)
        factors.append(factor)
        if step + 1 < NS_STEPS:
            turned = poly_one * gram + square_times(factor, gram_low)
            gram = poly_one * turned + square_times(turned.astype(low), factor)
    rows = raw_rows.shape[0]
    start = lax.axis_index("dp") * rows
    last = factors[-1]
    at = lax.broadcasted_iota(jnp.int32, (rows, D), 0) + start
    own = at == lax.broadcasted_iota(jnp.int32, (rows, D), 1)
    product = lax.dynamic_slice_in_dim(last, start, rows, axis=0).astype(jnp.float32)
    identity_part = poly_one
    for factor in factors[-2::-1]:
        product_low = product.astype(low)
        mine = lax.dynamic_slice_in_dim(factor, start, rows, axis=0).astype(jnp.float32)
        product = (
            poly_one * product + identity_part * mine + square_times(product_low, factor)
        )
        identity_part = identity_part * poly_one
    mapped = square_times(product.astype(low), raw)
    return ((identity_part * raw_rows.astype(jnp.float32) + mapped) * scale).astype(low)


def local(
    tokens_in,
    upstream,
    query_weight,
    key_weight,
    value_weight,
    gate_weight,
    output_weight,
    swiglu_gate,
    swiglu_up,
    swiglu_down,
    query_moment,
    key_moment,
    value_moment,
    gate_moment,
    output_moment,
    swiglu_gate_moment,
    swiglu_up_moment,
    swiglu_down_moment,
    small_params,
    small_moment,
):
    weights_in = (
        query_weight,
        key_weight,
        value_weight,
        gate_weight,
        output_weight,
        swiglu_gate,
        swiglu_up,
        swiglu_down,
    )
    moments_in = (
        query_moment,
        key_moment,
        value_moment,
        gate_moment,
        output_moment,
        swiglu_gate_moment,
        swiglu_up_moment,
        swiglu_down_moment,
    )
    low = jnp.bfloat16
    ctx_count = lax.axis_size("ctx")
    gain_one, gain_two, head_gain, conv_taps, decay_log, decay_bias, route_weight = unpack_small(
        small_params
    )
    route_low = route_weight.astype(low)
    rim_rows = CONV - 1
    front_rows = jnp.concatenate([member.astype(low) for member in weights_in[:4]], axis=1)
    back_rows = jnp.concatenate([member.astype(low) for member in weights_in[4:]], axis=1)
    front_full = lax.all_gather(front_rows, BOTH_AXES, axis=0, tiled=True)
    front_full, back_rows = lax.optimization_barrier((front_full, back_rows))
    back_full = lax.all_gather(back_rows, BOTH_AXES, axis=0, tiled=True)
    output_full = back_full[:, :VD]
    gate_up_full = back_full[:, VD : VD + 2 * FF]
    down_full = back_full[:, VD + 2 * FF :]

    inputs_full = tokens_in[0].astype(jnp.float32)
    normed_one, norm_one_back = jax.vjp(root_norm, inputs_full, gain_one)
    normed_one_low = normed_one.astype(low)
    projected = matmul(normed_one_low, front_full)
    pre_proj = projected[:, :QKV]
    route_pre = matmul(normed_one_low, route_low)
    prior_rim = passed_along(
        pre_proj[pre_proj.shape[0] - rim_rows :].astype(low), "ctx", 1
    ).astype(jnp.float32)
    extended = jnp.concatenate([prior_rim, pre_proj], axis=0)
    conv_out, conv_back = jax.vjp(conv_silu, extended, conv_taps)
    rates, rates_back = jax.vjp(rate_parts, route_pre, decay_log, decay_bias)
    gain_row = head_gain[None]

    inverse, both, maps = run_terms(conv_out, rates)
    trans, offset = maps[:, :, :DK], maps[:, :, DK:]
    levels, near_trans = window_maps(trans, 1)
    state_in = carried_state(levels, near_trans, offset, 1)
    back_levels, back_near = window_maps(jnp.swapaxes(trans, 1, 2), -1)
    mixed_low = run_outputs(conv_out, rates, both, projected, gain_row, state_in)
    residual_one = inputs_full + times_transposed(mixed_low, output_full)
    normed_two, norm_two_back = jax.vjp(root_norm, residual_one, gain_two)
    normed_two_low = normed_two.astype(low)
    gate_up = matmul(normed_two_low, gate_up_full)
    gate_act, up_act = gate_up[:, :FF], gate_up[:, FF:]
    sigma = jax.nn.sigmoid(gate_act)
    middle = (gate_act * sigma * up_act).astype(low)
    block_out = residual_one + times_transposed(middle, down_full)

    upstream_full = upstream[0]
    upstream_low = upstream_full.astype(low)
    grad_middle = matmul(upstream_low, down_full)
    grad_gate = (grad_middle * up_act * sigma * (1.0 + gate_act * (1.0 - sigma))).astype(low)
    grad_up = (grad_middle * gate_act * sigma).astype(low)
    grad_gate_up = jnp.concatenate([grad_gate, grad_up], axis=1)
    grad_normed_two = times_transposed(grad_gate_up, gate_up_full)
    grad_residual_norm, grad_gain_two = norm_two_back(grad_normed_two)
    grad_residual = upstream_full + grad_residual_norm
    grad_residual_low = grad_residual.astype(low)
    grad_mixed = matmul(grad_residual_low, output_full)

    early_left = jnp.concatenate([normed_one_low, upstream_low], axis=1)
    early_left, unused_full = lax.optimization_barrier((early_left, back_full))
    early_left = lax.all_gather(early_left, "ctx", axis=0, tiled=True)
    late_left = lax.all_gather(
        jnp.concatenate([normed_two_low, grad_residual_low], axis=1), "ctx", axis=0, tiled=True
    )

    state_grad = run_state(conv_out, rates, both, projected, gain_row, state_in, grad_mixed)
    state_out_grad = carried_state(back_levels, back_near, state_grad, -1)
    back_columns = jnp.concatenate(
        [swap_columns(member, ctx_count) for member in (mixed_low, grad_gate_up, middle)], axis=2
    )
    back_columns = lax.all_to_all(back_columns, "ctx", split_axis=0, concat_axis=0, tiled=True)

    query_grad, key_grad, value_grad, rates_grad, grad_gate_pre_low, gain_grads = run_backward(
        inverse, state_in, conv_out, rates, projected, gain_row, grad_mixed, state_out_grad
    )
    grad_conv = jnp.concatenate([query_grad, key_grad, value_grad], axis=1)
    grad_extended, grad_conv_taps = conv_back(grad_conv)
    grad_route_pre, grad_decay_log, grad_decay_bias = rates_back(rates_grad)
    grad_head_gain = jnp.sum(gain_grads, axis=(0, 1))
    back_rim = passed_along(shortened(grad_extended[:rim_rows]), "ctx", -1)
    grad_pre = grad_extended[rim_rows:]
    split_row = grad_pre.shape[0] - rim_rows
    grad_pre = jnp.concatenate([grad_pre[:split_row], grad_pre[split_row:] + back_rim], axis=0)
    grad_front_low = jnp.concatenate([grad_pre.astype(low), grad_gate_pre_low], axis=1)
    grad_route_low = grad_route_pre.astype(low)

    front_columns = lax.all_to_all(
        swap_columns(grad_front_low, ctx_count), "ctx", split_axis=0, concat_axis=0, tiled=True
    )
    count_rows = ctx_count * grad_front_low.shape[0]
    widths = (VD // ctx_count, 2 * FF // ctx_count, FF // ctx_count)
    back_columns = back_columns.reshape(count_rows, sum(widths))
    piece_out = back_columns[:, : widths[0]]
    piece_gate_up = back_columns[:, widths[0] : widths[0] + widths[1]]
    piece_down = back_columns[:, widths[0] + widths[1] :]
    back_terms = jnp.concatenate(
        [
            transposed_times(late_left[:, D:], piece_out).astype(low),
            transposed_times(late_left[:, :D], piece_gate_up).astype(low),
            transposed_times(early_left[:, D:], piece_down).astype(low),
        ],
        axis=1,
    )
    back_blocks = summed_rows(back_terms, sum(widths))
    front_width = grad_front_low.shape[1] // ctx_count
    front_terms = transposed_times(
        early_left[:, :D], front_columns.reshape(count_rows, front_width)
    ).astype(low)
    front_blocks = summed_rows(front_terms, front_width)
    front_grads = joined_columns(front_blocks)
    gate_up_grads = joined_columns(back_blocks[:, :, widths[0] : widths[0] + widths[1]])
    gradients = (
        front_grads[:, :KD],
        front_grads[:, KD : 2 * KD],
        front_grads[:, 2 * KD : QKV],
        front_grads[:, QKV:],
        joined_columns(back_blocks[:, :, : widths[0]]),
        gate_up_grads[:, :FF],
        gate_up_grads[:, FF:],
        joined_columns(back_blocks[:, :, widths[0] + widths[1] :]),
    )

    route_weight_grad = transposed_times(normed_one_low, grad_route_low)
    grad_normed_one = times_transposed(grad_front_low, front_full) + times_transposed(
        grad_route_low, route_low
    )
    grad_inputs, grad_gain_one = norm_one_back(grad_normed_one)
    input_grad = grad_residual + grad_inputs
    small_local = pack_small(
        (
            grad_gain_one,
            grad_gain_two,
            grad_head_gain,
            grad_conv_taps,
            grad_decay_log,
            grad_decay_bias,
            route_weight_grad,
        )
    )
    moments_new = tuple(
        (moment_rate * moment + gradient for moment, gradient in zip(moments_in, gradients))
    )
    squares_local = jnp.stack([jnp.sum(member * member) for member in moments_new])

    repeats = ctx_count // 8
    outgoing = jnp.stack(
        [
            jnp.pad(moments_new[owner // repeats].astype(low), ((0, 0), (0, FF - moments_new[owner // repeats].shape[1])))
            for owner in range(ctx_count)
        ]
    )
    received = lax.all_to_all(outgoing, "ctx", split_axis=0, concat_axis=0, tiled=True)
    ortho = orthogonal_rows(received.reshape(-1, FF))
    returned = lax.all_to_all(
        ortho.reshape(received.shape), "ctx", split_axis=0, concat_axis=0, tiled=True
    )
    weights_new = []
    for index in range(8):
        columns_now = weights_in[index].shape[1]
        factor = matrix_rate * math.sqrt(max(1.0, columns_now / D))
        weights_new.append(
            weights_in[index]
            - factor * returned[index * repeats, :, :columns_now].astype(jnp.float32)
        )
    summed = summed_everywhere(jnp.concatenate([small_local, squares_local]))
    small_grad = summed[: small_local.shape[0]]
    moment_norms = jnp.sqrt(summed[small_local.shape[0] :])
    small_moment_new = moment_rate * small_moment + small_grad
    small_new = small_params - small_rate * small_moment_new
    return (
        block_out[None],
        input_grad[None],
        *gradients,
        *weights_new,
        *moments_new,
        small_grad,
        small_new,
        small_moment_new,
        moment_norms,
    )


def solution(mesh):
    in_specs = (
        P("dp", "ctx", None),
        P("dp", "ctx", None),
        P(("dp", "ctx"), None),
        P(("dp", "ctx"), None),
        P(("dp", "ctx"), None),
        P(("dp", "ctx"), None),
        P(("dp", "ctx"), None),
        P(("dp", "ctx"), None),
        P(("dp", "ctx"), None),
        P(("dp", "ctx"), None),
        P(("dp", "ctx"), None),
        P(("dp", "ctx"), None),
        P(("dp", "ctx"), None),
        P(("dp", "ctx"), None),
        P(("dp", "ctx"), None),
        P(("dp", "ctx"), None),
        P(("dp", "ctx"), None),
        P(("dp", "ctx"), None),
        P(),
        P(),
    )
    out_specs = (
        P("dp", "ctx", None),
        P("dp", "ctx", None),
        P(("dp", "ctx"), None),
        P(("dp", "ctx"), None),
        P(("dp", "ctx"), None),
        P(("dp", "ctx"), None),
        P(("dp", "ctx"), None),
        P(("dp", "ctx"), None),
        P(("dp", "ctx"), None),
        P(("dp", "ctx"), None),
        P(("dp", "ctx"), None),
        P(("dp", "ctx"), None),
        P(("dp", "ctx"), None),
        P(("dp", "ctx"), None),
        P(("dp", "ctx"), None),
        P(("dp", "ctx"), None),
        P(("dp", "ctx"), None),
        P(("dp", "ctx"), None),
        P(("dp", "ctx"), None),
        P(("dp", "ctx"), None),
        P(("dp", "ctx"), None),
        P(("dp", "ctx"), None),
        P(("dp", "ctx"), None),
        P(("dp", "ctx"), None),
        P(("dp", "ctx"), None),
        P(("dp", "ctx"), None),
        P(),
        P(),
        P(),
        P(),
    )
    return jax.shard_map(local, mesh=mesh, in_specs=in_specs, out_specs=out_specs, check_vma=False)
```

```python
import math

import jax
import jax.numpy as jnp
from jax import lax
from jax.experimental import pallas as pl
from jax.sharding import Mesh, PartitionSpec as P

D = 1024
H = 6
DK = 128
DV = 256
CONV = 4
GROUP = 64
NS_STEPS = 3
KD = 768
VD = 1536
QKV = 3072
FF = 2816
DP_AXES = ("y", "core")
CTX_AXES = ("z", "x")
ALL_AXES = ("y", "core", "z", "x")
NEAR_AXES = ("core", "y", "x")
CHIP_AXES = ("y", "x")


highest_precision = lax.Precision.HIGHEST
eps_norm = 1e-05
eps_unit = 1e-06
eps_muon = 1e-07
moment_rate = 0.95
matrix_rate = 0.3
small_rate = 0.002
poly_one = 3.4445
poly_two = -4.775
poly_three = 2.0315


def passed_along(value, axis, steps):
    count = lax.axis_size(axis)
    first, last = (max(0, -steps), min(count, count - steps))
    return lax.ppermute(value, axis, [(source, source + steps) for source in range(first, last)])


def shortened(array):
    return jax.tree.map(lambda a: a.astype(jnp.bfloat16) if a.dtype == jnp.float32 else a, array)


def matmul(left, right):
    return jnp.dot(left, right, preferred_element_type=jnp.float32)


def times_transposed(left, right):
    return lax.dot_general(
        left, right, (((1,), (1,)), ((), ())), preferred_element_type=jnp.float32
    )


def transposed_times(left, right):
    return lax.dot_general(
        left, right, (((0,), (0,)), ((), ())), preferred_element_type=jnp.float32
    )


def root_norm(values, gain):
    return values * lax.rsqrt(jnp.mean(values * values, axis=-1, keepdims=True) + eps_norm) * gain


def unpack_small(packed):
    lengths = [D, D, DV, CONV * QKV, H, H, D * 2 * H]
    pieces = []
    offset = 0
    for length in lengths:
        pieces.append(packed[offset : offset + length])
        offset = offset + length
    return (
        pieces[0],
        pieces[1],
        pieces[2],
        pieces[3].reshape(CONV, QKV),
        pieces[4],
        pieces[5],
        pieces[6].reshape(D, 2 * H),
    )


def pack_small(members):
    return jnp.concatenate([member.reshape(-1) for member in members])


def conv_silu(extended, conv_taps):
    kernel_size = conv_taps.shape[0]
    rows_out = extended.shape[0] - kernel_size + 1
    summed = jnp.zeros((rows_out, extended.shape[1]), jnp.float32)
    for offset in range(kernel_size):
        summed = summed + conv_taps[offset] * extended[offset : offset + rows_out]
    return jax.nn.silu(summed)


def split_low(value):
    high = value.astype(jnp.bfloat16)
    return high, (value - high.astype(jnp.float32)).astype(jnp.bfloat16)


def raw_dot(left, right, left_dim, right_dim):
    def product(first, second):
        return lax.dot_general(
            first,
            second,
            (((left_dim,), (right_dim,)), ((), ())),
            preferred_element_type=jnp.float32,
        )

    left_high, left_rest = split_low(left)
    right_high, right_rest = split_low(right)
    return product(left_high, right_high) + (
        product(left_high, right_rest) + product(left_rest, right_high)
    )


@jax.custom_vjp
def mm(left, right):
    return raw_dot(left, right, 1, 0)


@jax.custom_vjp
def mm_nt(left, right):
    return raw_dot(left, right, 1, 1)


@jax.custom_vjp
def mm_tn(left, right):
    return raw_dot(left, right, 0, 0)


def keep_operands(function):
    return lambda left, right: (function(left, right), (left, right))


mm.defvjp(
    keep_operands(mm),
    lambda kept, grad: (raw_dot(grad, kept[1], 1, 1), raw_dot(kept[0], grad, 0, 0)),
)
mm_nt.defvjp(
    keep_operands(mm_nt),
    lambda kept, grad: (raw_dot(grad, kept[1], 1, 0), raw_dot(grad, kept[0], 0, 0)),
)
mm_tn.defvjp(
    keep_operands(mm_tn),
    lambda kept, grad: (raw_dot(kept[1], grad, 1, 1), raw_dot(kept[0], grad, 1, 0)),
)


def position_pair(rows, columns):
    return (
        lax.broadcasted_iota(jnp.int32, (rows, columns), 0),
        lax.broadcasted_iota(jnp.int32, (rows, columns), 1),
    )


def widened(member, columns):
    copies = columns // member.shape[1]
    return member if copies == 1 else jnp.concatenate([member] * copies, axis=1)


def head_masks(rows):
    at, source = position_pair(rows, rows)
    same = at // GROUP == source // GROUP
    return same, same & (at >= source), same & (at > source)


def unit_inverse(lower):
    rows = lower.shape[0]
    at, source = position_pair(rows, rows)

    def step_part(block):
        inside = (at // (2 * block) == source // (2 * block)) & (at // block != source // block)
        return jnp.where(inside, lower, 0.0)

    result = jnp.where(at == source, 1.0, 0.0) - step_part(1)
    block = 2
    while block < GROUP:
        result = result - raw_dot(result, raw_dot(step_part(block), result, 1, 0), 1, 0)
        block = 2 * block
    return result


@jax.custom_vjp
def solved(lower, target, inverse):
    return raw_dot(inverse, target, 1, 0)


def solved_forward(lower, target, inverse):
    result = raw_dot(inverse, target, 1, 0)
    return (result, (inverse, result))


def solved_backward(kept, grad):
    inverse, result = kept
    target_grad = raw_dot(inverse, grad, 0, 0)
    return (-raw_dot(target_grad, result, 1, 1), target_grad, jnp.zeros_like(inverse))


solved.defvjp(solved_forward, solved_backward)


def decay_parts(log_wide):
    rows = log_wide.shape[0]
    at, source = position_pair(rows, rows)
    same, inclusive, _ = head_masks(rows)
    growth = jnp.exp(mm(inclusive.astype(jnp.float32), log_wide))
    tail = jnp.exp(mm((same & ~inclusive).astype(jnp.float32), log_wide))
    differ = mm(inclusive.astype(jnp.float32), jnp.where(at > source, log_wide, 0.0))
    within = jnp.where(inclusive, jnp.exp(jnp.where(inclusive, differ, 0.0)), 0.0)
    return growth, tail, within


def group_decay(log_wide, group):
    rows = log_wide.shape[0]
    source = lax.broadcasted_iota(jnp.int32, (DK, rows), 1)
    return jnp.exp(mm((source // GROUP == group).astype(jnp.float32), log_wide))


def in_group(member, group):
    row = lax.broadcasted_iota(jnp.int32, member.shape, 0)
    return jnp.where(row // GROUP == group, member, 0.0)


def lower_system(keys, beta_wide, within):
    _, _, strictly = head_masks(keys.shape[0])
    return jnp.where(strictly, beta_wide * within * mm_nt(keys, keys), 0.0)


def solve_targets(keys, values, beta_wide, growth):
    return jnp.concatenate(
        [beta_wide * growth * keys, widened(beta_wide, DV) * values], axis=1
    )


def head_terms(keys, values, beta_wide, log_wide):
    growth, tail, within = decay_parts(log_wide)
    lower = lower_system(keys, beta_wide, within)
    inverse = unit_inverse(lower)
    both = raw_dot(inverse, solve_targets(keys, values, beta_wide, growth), 1, 0)
    solved_keys = both[:, :DK]
    at, source = position_pair(DK, DK + DV)
    state = jnp.where(at == source, 1.0, 0.0)
    offset_rows = jnp.where(
        lax.broadcasted_iota(jnp.int32, both.shape, 1) >= DK, both, 0.0
    )
    decayed_keys = keys * tail
    for group in range(keys.shape[0] // GROUP):
        pseudo = offset_rows - mm(solved_keys, state)
        state = widened(group_decay(log_wide, group), DK + DV) * state + mm_tn(
            in_group(decayed_keys, group), pseudo
        )
    return inverse, both, state


def head_outputs(queries, keys, log_wide, both, gate_pre, head_gain, state):
    growth, tail, within = decay_parts(log_wide)
    attend = within * mm_nt(queries, keys)
    decayed_keys = keys * tail
    solved_keys, solved_values = both[:, :DK], both[:, DK:]
    stacked = jnp.concatenate([queries, solved_keys], axis=0)
    rows = queries.shape[0]
    read = 0.0
    for group in range(rows // GROUP):
        now = mm(stacked, state)
        pseudo_now = solved_values - now[rows:]
        read = read + jnp.concatenate(
            [in_group(now[:rows], group), in_group(now[rows:], group)], axis=0
        )
        state = widened(group_decay(log_wide, group), DV) * state + mm_tn(
            in_group(decayed_keys, group), pseudo_now
        )
    output_rows = widened(growth, DV) * read[:rows] + mm(attend, solved_values - read[rows:])
    normed = (
        output_rows
        * lax.rsqrt(jnp.mean(output_rows * output_rows, axis=-1, keepdims=True) + eps_norm)
        * head_gain
    )
    return normed * (gate_pre * jax.nn.sigmoid(gate_pre)), state


def head_whole(inverse, state, queries, keys, values, beta_wide, log_wide, gate_pre, head_gain):
    growth, _, within = decay_parts(log_wide)
    lower = lower_system(keys, beta_wide, within)
    both = solved(lower, solve_targets(keys, values, beta_wide, growth), inverse)
    return head_outputs(queries, keys, log_wide, both, gate_pre, head_gain, state)


def unit_rows_scaled(values, factor):
    return values * lax.rsqrt(jnp.sum(values * values, axis=-1, keepdims=True) + eps_unit) * factor


def rate_columns(rates, head):
    lane = lax.broadcasted_iota(jnp.int32, rates.shape, 1)
    beta = jnp.sum(jnp.where(lane == head, rates, 0.0), axis=1, keepdims=True)
    log_decay = jnp.sum(jnp.where(lane == head + H, rates, 0.0), axis=1, keepdims=True)
    wide = (rates.shape[0], DK)
    return jnp.broadcast_to(beta, wide), jnp.broadcast_to(log_decay, wide)


def head_inputs(query_conv, key_conv, rates, head):
    queries = unit_rows_scaled(query_conv, DK ** (-0.5))
    keys = unit_rows_scaled(key_conv, 1.0)
    beta_wide, log_wide = rate_columns(rates, head)
    return queries, keys, beta_wide, log_wide


def terms_kernel(query_ref, key_ref, value_ref, rates_ref, inverse_ref, both_ref, map_ref):
    _, keys, beta_wide, log_wide = head_inputs(
        query_ref[...], key_ref[...], rates_ref[...], pl.program_id(0)
    )
    inverse, both, state = head_terms(keys, value_ref[...], beta_wide, log_wide)
    inverse_ref[...] = inverse
    both_ref[...] = both
    map_ref[0] = state


def outputs_kernel(
    query_ref, key_ref, rates_ref, both_ref, gate_ref, gain_ref, state_ref, mixed_ref
):
    queries, keys, _, log_wide = head_inputs(
        query_ref[...], key_ref[...], rates_ref[...], pl.program_id(0)
    )
    mixed, _ = head_outputs(
        queries, keys, log_wide, both_ref[...], gate_ref[...], gain_ref[...], state_ref[0]
    )
    mixed_ref[...] = mixed.astype(mixed_ref.dtype)


def state_kernel(
    query_ref, key_ref, rates_ref, both_ref, gate_ref, gain_ref, state_ref, grad_ref, out_ref
):
    queries, keys, _, log_wide = head_inputs(
        query_ref[...], key_ref[...], rates_ref[...], pl.program_id(0)
    )

    def from_state(state):
        return head_outputs(
            queries, keys, log_wide, both_ref[...], gate_ref[...], gain_ref[...], state
        )[0]

    _, back = jax.vjp(from_state, state_ref[0])
    out_ref[0] = back(grad_ref[...])[0]


def backward_kernel(
    inverse_ref,
    state_ref,
    query_ref,
    key_ref,
    value_ref,
    rates_ref,
    gate_ref,
    gain_ref,
    grad_ref,
    state_grad_ref,
    query_out,
    key_out,
    value_out,
    rates_out,
    gate_out,
    gain_out,
):
    inverse, state = inverse_ref[...], state_ref[0]
    head = pl.program_id(0)

    def whole(query_conv, key_conv, values, rates, gate_pre, gain):
        queries, keys, beta_wide, log_wide = head_inputs(query_conv, key_conv, rates, head)
        return head_whole(
            inverse, state, queries, keys, values, beta_wide, log_wide, gate_pre, gain
        )

    _, back = jax.vjp(
        whole,
        query_ref[...],
        key_ref[...],
        value_ref[...],
        rates_ref[...],
        gate_ref[...],
        gain_ref[...],
    )
    grads = back((grad_ref[...], state_grad_ref[0]))
    query_out[...] = grads[0]
    key_out[...] = grads[1]
    value_out[...] = grads[2]
    gate_out[...] = grads[4].astype(gate_out.dtype)
    gain_out[0] = grads[5]

    @pl.when(head == 0)
    def first_head():
        rates_out[...] = grads[3]

    @pl.when(head > 0)
    def later_head():
        rates_out[...] = rates_out[...] + grads[3]


def columns_of(rows, width, first=0):
    return pl.BlockSpec((rows, width), lambda head: (0, head + first))


def matrix_of(rows, width):
    return pl.BlockSpec((1, rows, width), lambda head: (head, 0, 0))


def fixed_block(rows, width):
    return pl.BlockSpec((rows, width), lambda head: (0, 0))


def per_head(kernel, in_specs, out_specs, out_shapes):
    return pl.pallas_call(
        kernel, grid=(H,), in_specs=in_specs, out_specs=out_specs, out_shape=out_shapes
    )


def shape_of(*dims, kind=jnp.float32):
    return jax.ShapeDtypeStruct(dims, kind)


def run_terms(conv_out, rates):
    rows = conv_out.shape[0]
    return per_head(
        terms_kernel,
        [
            columns_of(rows, DK),
            columns_of(rows, DK, H),
            columns_of(rows, DV, 2 * KD // DV),
            fixed_block(rows, 2 * H),
        ],
        [columns_of(rows, rows), columns_of(rows, DK + DV), matrix_of(DK, DK + DV)],
        [
            shape_of(rows, H * rows),
            shape_of(rows, H * (DK + DV)),
            shape_of(H, DK, DK + DV),
        ],
    )(conv_out, conv_out, conv_out, rates)


def output_specs(rows):
    return [
        columns_of(rows, DK),
        columns_of(rows, DK, H),
        fixed_block(rows, 2 * H),
        columns_of(rows, DK + DV),
        columns_of(rows, DV, QKV // DV),
        fixed_block(1, DV),
        matrix_of(DK, DV),
    ]


def run_outputs(conv_out, rates, both, projected, gain_row, state):
    rows = conv_out.shape[0]
    return per_head(
        outputs_kernel,
        output_specs(rows),
        columns_of(rows, DV),
        shape_of(rows, H * DV, kind=jnp.bfloat16),
    )(conv_out, conv_out, rates, both, projected, gain_row, state)


def run_state(conv_out, rates, both, projected, gain_row, state, grad):
    rows = conv_out.shape[0]
    return per_head(
        state_kernel,
        output_specs(rows) + [columns_of(rows, DV)],
        matrix_of(DK, DV),
        shape_of(H, DK, DV),
    )(conv_out, conv_out, rates, both, projected, gain_row, state, grad)


def run_backward(inverse, state, conv_out, rates, projected, gain_row, grad, state_grad):
    rows = conv_out.shape[0]
    narrow, wide = columns_of(rows, DK), columns_of(rows, DV)
    return per_head(
        backward_kernel,
        [
            columns_of(rows, rows),
            matrix_of(DK, DV),
            narrow,
            columns_of(rows, DK, H),
            columns_of(rows, DV, 2 * KD // DV),
            fixed_block(rows, 2 * H),
            columns_of(rows, DV, QKV // DV),
            fixed_block(1, DV),
            wide,
            matrix_of(DK, DV),
        ],
        [narrow, narrow, wide, fixed_block(rows, 2 * H), wide, matrix_of(1, DV)],
        [
            shape_of(rows, H * DK),
            shape_of(rows, H * DK),
            shape_of(rows, H * DV),
            shape_of(rows, 2 * H),
            shape_of(rows, H * DV, kind=jnp.bfloat16),
            shape_of(H, 1, DV),
        ],
    )(
        inverse,
        state,
        conv_out,
        conv_out,
        conv_out,
        rates,
        projected,
        gain_row,
        grad,
        state_grad,
    )


def rate_parts(route_pre, decay_log, decay_bias):
    betas = jax.nn.sigmoid(route_pre[:, :H])
    log_decay = -jnp.exp(decay_log) * jax.nn.softplus(route_pre[:, H:] + decay_bias)
    return jnp.concatenate([betas, log_decay], axis=1)


def map_times(left, right):
    return jnp.einsum("hij,hjv->hiv", left, right, precision=highest_precision)


def sent_low(value, steps):
    return passed_along(value.astype(jnp.bfloat16), CTX_AXES, steps).astype(jnp.float32)


def window_maps(trans, direction):
    count = lax.axis_size(CTX_AXES)
    levels = [trans]
    window = 1
    while 2 * window < count:
        levels.append(map_times(levels[-1], sent_low(levels[-1], direction * window)))
        window = 2 * window
    return levels, sent_low(levels[-1], direction)


def carried_state(levels, near_trans, offset, direction):
    window = 1
    for trans in levels[:-1]:
        before = sent_low(offset, direction * window)
        offset = offset + map_times(trans, before)
        window = 2 * window
    near = sent_low(offset, direction)
    far = sent_low(offset, direction * (window + 1))
    return near + map_times(near_trans, far)


def swap_columns(rows, count):
    split = rows.reshape(rows.shape[0], count, rows.shape[1] // count)
    return jnp.transpose(split, (1, 0, 2))


def gathered_near(rows):
    chips = lax.axis_size(CHIP_AXES)
    own = lax.all_to_all(
        jnp.broadcast_to(rows[None], (chips,) + rows.shape),
        CHIP_AXES,
        split_axis=0,
        concat_axis=0,
        tiled=True,
    )
    own = own.reshape(-1, rows.shape[1])
    other = lax.ppermute(own, "core", [(0, 1), (1, 0)])
    first = lax.axis_index("core") == 0
    return jnp.concatenate([jnp.where(first, own, other), jnp.where(first, other, own)], axis=0)


def summed_rows(terms, columns):
    y_count, core_count, far_count, x_count = (lax.axis_size(axis) for axis in ALL_AXES)
    near_count = lax.axis_size(NEAR_AXES)
    rows = D // far_count
    split = terms.reshape(
        y_count, core_count, far_count, x_count, rows // near_count, columns
    )
    split = jnp.transpose(split, (2, 1, 0, 3, 4, 5)).reshape(far_count, rows, columns)
    mine = lax.axis_index("z")
    total = lax.dynamic_index_in_dim(split, mine, 0, keepdims=False).astype(jnp.float32)
    for step in range(1, far_count):
        pairs = [(source, (source + step) % far_count) for source in range(far_count)]
        leaving = lax.dynamic_index_in_dim(split, (mine + step) % far_count, 0, keepdims=False)
        arrived = lax.ppermute(leaving, "z", pairs)
        total = total + arrived.astype(jnp.float32)
    block = total.astype(jnp.bfloat16)
    return lax.all_to_all(
        block.reshape(near_count, rows // near_count, columns),
        NEAR_AXES,
        split_axis=0,
        concat_axis=0,
        tiled=True,
    )


def joined_columns(blocks):
    count, rows, columns = blocks.shape
    return jnp.transpose(blocks, (1, 0, 2)).reshape(rows, count * columns).astype(jnp.float32)


def summed_everywhere(vector):
    count = lax.axis_size(ALL_AXES)
    chunk = -(-vector.shape[0] // (count * 128)) * 128
    padded = jnp.pad(vector, (0, count * chunk - vector.shape[0])).reshape(count, chunk)
    parts = lax.all_to_all(padded, ALL_AXES, split_axis=0, concat_axis=0, tiled=True)
    total = jnp.broadcast_to(jnp.sum(parts, axis=0)[None], (count, chunk))
    whole = lax.all_to_all(total, ALL_AXES, split_axis=0, concat_axis=0, tiled=True)
    return whole.reshape(-1)[: vector.shape[0]]


def square_times(left, right):
    return jnp.dot(left, right, preferred_element_type=jnp.float32)


def orthogonal_rows(raw_rows):
    low = jnp.bfloat16
    raw = lax.all_gather(raw_rows, DP_AXES, axis=0, tiled=True)
    gram_raw = times_transposed(raw, raw)
    norm = jnp.sqrt(jnp.trace(gram_raw))
    scale = 1.0 / (norm + eps_muon)
    gram = gram_raw * (scale * scale)
    factors = []
    for step in range(NS_STEPS):
        gram_low = gram.astype(low)
        factor = (poly_two * gram + poly_three * square_times(gram_low, gram_low)).astype(low)
        factors.append(factor)
        if step + 1 < NS_STEPS:
            turned = poly_one * gram + square_times(factor, gram_low)
            gram = poly_one * turned + square_times(turned.astype(low), factor)
    rows = raw_rows.shape[0]
    start = lax.axis_index(DP_AXES) * rows
    last = factors[-1]
    at = lax.broadcasted_iota(jnp.int32, (rows, D), 0) + start
    own = at == lax.broadcasted_iota(jnp.int32, (rows, D), 1)
    product = lax.dynamic_slice_in_dim(last, start, rows, axis=0).astype(jnp.float32)
    identity_part = poly_one
    for factor in factors[-2::-1]:
        product_low = product.astype(low)
        mine = lax.dynamic_slice_in_dim(factor, start, rows, axis=0).astype(jnp.float32)
        product = (
            poly_one * product + identity_part * mine + square_times(product_low, factor)
        )
        identity_part = identity_part * poly_one
    mapped = square_times(product.astype(low), raw)
    return ((identity_part * raw_rows.astype(jnp.float32) + mapped) * scale).astype(low)


def local(
    tokens_in,
    upstream,
    query_weight,
    key_weight,
    value_weight,
    gate_weight,
    output_weight,
    swiglu_gate,
    swiglu_up,
    swiglu_down,
    query_moment,
    key_moment,
    value_moment,
    gate_moment,
    output_moment,
    swiglu_gate_moment,
    swiglu_up_moment,
    swiglu_down_moment,
    small_params,
    small_moment,
):
    weights_in = (
        query_weight,
        key_weight,
        value_weight,
        gate_weight,
        output_weight,
        swiglu_gate,
        swiglu_up,
        swiglu_down,
    )
    moments_in = (
        query_moment,
        key_moment,
        value_moment,
        gate_moment,
        output_moment,
        swiglu_gate_moment,
        swiglu_up_moment,
        swiglu_down_moment,
    )
    low = jnp.bfloat16
    ctx_count = lax.axis_size(CTX_AXES)
    near_count = lax.axis_size(NEAR_AXES)
    gain_one, gain_two, head_gain, conv_taps, decay_log, decay_bias, route_weight = unpack_small(
        small_params
    )
    route_low = route_weight.astype(low)
    rim_rows = CONV - 1
    front_rows = jnp.concatenate([member.astype(low) for member in weights_in[:4]], axis=1)
    back_rows = jnp.concatenate([member.astype(low) for member in weights_in[4:]], axis=1)
    front_full = lax.all_gather(front_rows, ALL_AXES, axis=0, tiled=True)
    front_full, back_rows = lax.optimization_barrier((front_full, back_rows))
    back_full = lax.all_gather(back_rows, ALL_AXES, axis=0, tiled=True)
    output_full = back_full[:, :VD]
    gate_up_full = back_full[:, VD : VD + 2 * FF]
    down_full = back_full[:, VD + 2 * FF :]

    inputs_full = tokens_in[0].astype(jnp.float32)
    normed_one, norm_one_back = jax.vjp(root_norm, inputs_full, gain_one)
    normed_one_low = normed_one.astype(low)
    upstream_full = upstream[0]
    upstream_low = upstream_full.astype(low)
    early_left = gathered_near(jnp.concatenate([normed_one_low, upstream_low], axis=1))
    projected = matmul(normed_one_low, front_full)
    pre_proj = projected[:, :QKV]
    route_pre = matmul(normed_one_low, route_low)
    prior_rim = passed_along(
        pre_proj[pre_proj.shape[0] - rim_rows :].astype(low), CTX_AXES, 1
    ).astype(jnp.float32)
    extended = jnp.concatenate([prior_rim, pre_proj], axis=0)
    conv_out, conv_back = jax.vjp(conv_silu, extended, conv_taps)
    rates, rates_back = jax.vjp(rate_parts, route_pre, decay_log, decay_bias)
    gain_row = head_gain[None]

    inverse, both, maps = run_terms(conv_out, rates)
    trans, offset = maps[:, :, :DK], maps[:, :, DK:]
    levels, near_trans = window_maps(trans, 1)
    state_in = carried_state(levels, near_trans, offset, 1)
    back_levels, back_near = window_maps(jnp.swapaxes(trans, 1, 2), -1)
    mixed_low = run_outputs(conv_out, rates, both, projected, gain_row, state_in)
    residual_one = inputs_full + times_transposed(mixed_low, output_full)
    normed_two, norm_two_back = jax.vjp(root_norm, residual_one, gain_two)
    normed_two_low = normed_two.astype(low)
    gate_up = matmul(normed_two_low, gate_up_full)
    gate_act, up_act = gate_up[:, :FF], gate_up[:, FF:]
    sigma = jax.nn.sigmoid(gate_act)
    middle = (gate_act * sigma * up_act).astype(low)
    block_out = residual_one + times_transposed(middle, down_full)

    grad_middle = matmul(upstream_low, down_full)
    grad_gate = (grad_middle * up_act * sigma * (1.0 + gate_act * (1.0 - sigma))).astype(low)
    grad_up = (grad_middle * gate_act * sigma).astype(low)
    grad_gate_up = jnp.concatenate([grad_gate, grad_up], axis=1)
    grad_normed_two = times_transposed(grad_gate_up, gate_up_full)
    grad_residual_norm, grad_gain_two = norm_two_back(grad_normed_two)
    grad_residual = upstream_full + grad_residual_norm
    grad_residual_low = grad_residual.astype(low)
    grad_mixed = matmul(grad_residual_low, output_full)

    late_left = gathered_near(jnp.concatenate([normed_two_low, grad_residual_low], axis=1))
    back_columns = jnp.concatenate(
        [swap_columns(member, near_count) for member in (mixed_low, grad_gate_up, middle)], axis=2
    )
    back_columns = lax.all_to_all(back_columns, NEAR_AXES, split_axis=0, concat_axis=0, tiled=True)
    state_grad = run_state(conv_out, rates, both, projected, gain_row, state_in, grad_mixed)
    state_out_grad = carried_state(back_levels, back_near, state_grad, -1)

    (query_grad, key_grad, value_grad, rates_grad, grad_gate_pre_low, gain_grads) = run_backward(
        inverse, state_in, conv_out, rates, projected, gain_row, grad_mixed, state_out_grad
    )
    grad_conv = jnp.concatenate([query_grad, key_grad, value_grad], axis=1)
    grad_extended, grad_conv_taps = conv_back(grad_conv)
    grad_route_pre, grad_decay_log, grad_decay_bias = rates_back(rates_grad)
    grad_head_gain = jnp.sum(gain_grads, axis=(0, 1))
    back_rim = passed_along(shortened(grad_extended[:rim_rows]), CTX_AXES, -1)
    grad_pre = grad_extended[rim_rows:]
    split_row = grad_pre.shape[0] - rim_rows
    grad_pre = jnp.concatenate([grad_pre[:split_row], grad_pre[split_row:] + back_rim], axis=0)
    grad_front_low = jnp.concatenate([grad_pre.astype(low), grad_gate_pre_low], axis=1)
    grad_route_low = grad_route_pre.astype(low)

    front_columns = lax.all_to_all(
        swap_columns(grad_front_low, near_count),
        NEAR_AXES,
        split_axis=0,
        concat_axis=0,
        tiled=True,
    )
    count_rows = near_count * grad_front_low.shape[0]
    widths = (VD // near_count, 2 * FF // near_count, FF // near_count)
    back_columns = back_columns.reshape(count_rows, sum(widths))
    piece_out = back_columns[:, : widths[0]]
    piece_gate_up = back_columns[:, widths[0] : widths[0] + widths[1]]
    piece_down = back_columns[:, widths[0] + widths[1] :]
    back_terms = jnp.concatenate(
        [
            transposed_times(late_left[:, D:], piece_out).astype(low),
            transposed_times(late_left[:, :D], piece_gate_up).astype(low),
            transposed_times(early_left[:, D:], piece_down).astype(low),
        ],
        axis=1,
    )
    back_blocks = summed_rows(back_terms, sum(widths))
    front_width = grad_front_low.shape[1] // near_count
    front_terms = transposed_times(
        early_left[:, :D], front_columns.reshape(count_rows, front_width)
    ).astype(low)
    front_blocks = summed_rows(front_terms, front_width)
    front_grads = joined_columns(front_blocks)
    gate_up_grads = joined_columns(back_blocks[:, :, widths[0] : widths[0] + widths[1]])
    gradients = (
        front_grads[:, :KD],
        front_grads[:, KD : 2 * KD],
        front_grads[:, 2 * KD : QKV],
        front_grads[:, QKV:],
        joined_columns(back_blocks[:, :, : widths[0]]),
        gate_up_grads[:, :FF],
        gate_up_grads[:, FF:],
        joined_columns(back_blocks[:, :, widths[0] + widths[1] :]),
    )

    route_weight_grad = transposed_times(normed_one_low, grad_route_low)
    grad_normed_one = times_transposed(grad_front_low, front_full) + times_transposed(
        grad_route_low, route_low
    )
    grad_inputs, grad_gain_one = norm_one_back(grad_normed_one)
    input_grad = grad_residual + grad_inputs
    small_local = pack_small(
        (
            grad_gain_one,
            grad_gain_two,
            grad_head_gain,
            grad_conv_taps,
            grad_decay_log,
            grad_decay_bias,
            route_weight_grad,
        )
    )
    moments_new = tuple(
        (moment_rate * moment + gradient for moment, gradient in zip(moments_in, gradients))
    )
    squares_local = jnp.stack([jnp.sum(member * member) for member in moments_new])

    repeats = ctx_count // 8
    outgoing = jnp.stack(
        [
            jnp.pad(moments_new[owner // repeats].astype(low), ((0, 0), (0, FF - moments_new[owner // repeats].shape[1])))
            for owner in range(ctx_count)
        ]
    )
    received = lax.all_to_all(outgoing, CTX_AXES, split_axis=0, concat_axis=0, tiled=True)
    ortho = orthogonal_rows(received.reshape(-1, FF))
    returned = lax.all_to_all(
        ortho.reshape(received.shape), CTX_AXES, split_axis=0, concat_axis=0, tiled=True
    )
    weights_new = []
    for index in range(8):
        columns_now = weights_in[index].shape[1]
        factor = matrix_rate * math.sqrt(max(1.0, columns_now / D))
        weights_new.append(
            weights_in[index]
            - factor * returned[index * repeats, :, :columns_now].astype(jnp.float32)
        )
    summed = summed_everywhere(jnp.concatenate([small_local, squares_local]))
    small_grad = summed[: small_local.shape[0]]
    moment_norms = jnp.sqrt(summed[small_local.shape[0] :])
    small_moment_new = moment_rate * small_moment + small_grad
    small_new = small_params - small_rate * small_moment_new
    return (
        block_out[None],
        input_grad[None],
        *gradients,
        *weights_new,
        *moments_new,
        small_grad,
        small_new,
        small_moment_new,
        moment_norms,
    )


def solution(mesh):
    dp_count, ctx_count = mesh.shape["dp"], mesh.shape["ctx"]
    split_mesh = Mesh(mesh.devices.reshape(dp_count // 2, 2, ctx_count // 2, 2), ALL_AXES)
    tokens, rows, copied = P(DP_AXES, CTX_AXES, None), P(ALL_AXES, None), P()
    in_specs = (tokens,) * 2 + (rows,) * 16 + (copied,) * 2
    out_specs = (tokens,) * 2 + (rows,) * 24 + (copied,) * 4

    return jax.shard_map(
        local, mesh=split_mesh, in_specs=in_specs, out_specs=out_specs, check_vma=False
    )
```

```python
import math

import jax
import jax.numpy as jnp
from jax import lax
from jax.experimental import pallas as pl
from jax.sharding import Mesh, PartitionSpec as P

D = 1024
H = 6
DK = 128
DV = 256
CONV = 4
GROUP = 64
NS_STEPS = 3
KD = 768
VD = 1536
QKV = 3072
FF = 2816
DP_AXES = ("y", "core")
CTX_AXES = ("z", "x")
ALL_AXES = ("y", "core", "z", "x")
NEAR_AXES = ("core", "y", "x")
CHIP_AXES = ("y", "x")


highest_precision = lax.Precision.HIGHEST
eps_norm = 1e-05
eps_unit = 1e-06
eps_muon = 1e-07
moment_rate = 0.95
matrix_rate = 0.3
small_rate = 0.002
poly_one = 3.4445
poly_two = -4.775
poly_three = 2.0315


def passed_along(value, axis, steps):
    count = lax.axis_size(axis)
    first, last = (max(0, -steps), min(count, count - steps))
    return lax.ppermute(value, axis, [(source, source + steps) for source in range(first, last)])


def shortened(array):
    return jax.tree.map(lambda a: a.astype(jnp.bfloat16) if a.dtype == jnp.float32 else a, array)


def matmul(left, right):
    return jnp.dot(left, right, preferred_element_type=jnp.float32)


def times_transposed(left, right):
    return lax.dot_general(
        left, right, (((1,), (1,)), ((), ())), preferred_element_type=jnp.float32
    )


def transposed_times(left, right):
    return lax.dot_general(
        left, right, (((0,), (0,)), ((), ())), preferred_element_type=jnp.float32
    )


def root_norm(values, gain):
    return values * lax.rsqrt(jnp.mean(values * values, axis=-1, keepdims=True) + eps_norm) * gain


def unpack_small(packed):
    lengths = [D, D, DV, CONV * QKV, H, H, D * 2 * H]
    pieces = []
    offset = 0
    for length in lengths:
        pieces.append(packed[offset : offset + length])
        offset = offset + length
    return (
        pieces[0],
        pieces[1],
        pieces[2],
        pieces[3].reshape(CONV, QKV),
        pieces[4],
        pieces[5],
        pieces[6].reshape(D, 2 * H),
    )


def pack_small(members):
    return jnp.concatenate([member.reshape(-1) for member in members])


def conv_silu(extended, conv_taps):
    kernel_size = conv_taps.shape[0]
    rows_out = extended.shape[0] - kernel_size + 1
    summed = jnp.zeros((rows_out, extended.shape[1]), jnp.float32)
    for offset in range(kernel_size):
        summed = summed + conv_taps[offset] * extended[offset : offset + rows_out]
    return jax.nn.silu(summed)


def split_low(value):
    high = value.astype(jnp.bfloat16)
    return high, (value - high.astype(jnp.float32)).astype(jnp.bfloat16)


def raw_dot(left, right, left_dim, right_dim):
    def product(first, second):
        return lax.dot_general(
            first,
            second,
            (((left_dim,), (right_dim,)), ((), ())),
            preferred_element_type=jnp.float32,
        )

    left_high, left_rest = split_low(left)
    right_high, right_rest = split_low(right)
    return product(left_high, right_high) + (
        product(left_high, right_rest) + product(left_rest, right_high)
    )


@jax.custom_vjp
def mm(left, right):
    return raw_dot(left, right, 1, 0)


@jax.custom_vjp
def mm_nt(left, right):
    return raw_dot(left, right, 1, 1)


@jax.custom_vjp
def mm_tn(left, right):
    return raw_dot(left, right, 0, 0)


def keep_operands(function):
    return lambda left, right: (function(left, right), (left, right))


mm.defvjp(
    keep_operands(mm),
    lambda kept, grad: (raw_dot(grad, kept[1], 1, 1), raw_dot(kept[0], grad, 0, 0)),
)
mm_nt.defvjp(
    keep_operands(mm_nt),
    lambda kept, grad: (raw_dot(grad, kept[1], 1, 0), raw_dot(grad, kept[0], 0, 0)),
)
mm_tn.defvjp(
    keep_operands(mm_tn),
    lambda kept, grad: (raw_dot(kept[1], grad, 1, 1), raw_dot(kept[0], grad, 1, 0)),
)


def position_pair(rows, columns):
    return (
        lax.broadcasted_iota(jnp.int32, (rows, columns), 0),
        lax.broadcasted_iota(jnp.int32, (rows, columns), 1),
    )


def widened(member, columns):
    copies = columns // member.shape[1]
    return member if copies == 1 else jnp.concatenate([member] * copies, axis=1)


def head_masks(rows):
    at, source = position_pair(rows, rows)
    same = at // GROUP == source // GROUP
    return same, same & (at >= source), same & (at > source)


def unit_inverse(lower):
    rows = lower.shape[0]
    at, source = position_pair(rows, rows)

    def step_part(block):
        inside = (at // (2 * block) == source // (2 * block)) & (at // block != source // block)
        return jnp.where(inside, lower, 0.0)

    result = jnp.where(at == source, 1.0, 0.0) - step_part(1)
    block = 2
    while block < GROUP:
        result = result - raw_dot(result, raw_dot(step_part(block), result, 1, 0), 1, 0)
        block = 2 * block
    return result


@jax.custom_vjp
def solved(lower, target, inverse):
    return raw_dot(inverse, target, 1, 0)


def solved_forward(lower, target, inverse):
    result = raw_dot(inverse, target, 1, 0)
    return (result, (inverse, result))


def solved_backward(kept, grad):
    inverse, result = kept
    target_grad = raw_dot(inverse, grad, 0, 0)
    return (-raw_dot(target_grad, result, 1, 1), target_grad, jnp.zeros_like(inverse))


solved.defvjp(solved_forward, solved_backward)


def decay_parts(log_wide):
    rows = log_wide.shape[0]
    at, source = position_pair(rows, rows)
    same, inclusive, _ = head_masks(rows)
    growth = jnp.exp(mm(inclusive.astype(jnp.float32), log_wide))
    tail = jnp.exp(mm((same & ~inclusive).astype(jnp.float32), log_wide))
    differ = mm(inclusive.astype(jnp.float32), jnp.where(at > source, log_wide, 0.0))
    within = jnp.where(inclusive, jnp.exp(jnp.where(inclusive, differ, 0.0)), 0.0)
    return growth, tail, within


def group_decay(log_wide, group):
    rows = log_wide.shape[0]
    source = lax.broadcasted_iota(jnp.int32, (DK, rows), 1)
    return jnp.exp(mm((source // GROUP == group).astype(jnp.float32), log_wide))


def in_group(member, group):
    row = lax.broadcasted_iota(jnp.int32, member.shape, 0)
    return jnp.where(row // GROUP == group, member, 0.0)


def lower_system(keys, beta_wide, within):
    _, _, strictly = head_masks(keys.shape[0])
    return jnp.where(strictly, beta_wide * within * mm_nt(keys, keys), 0.0)


def solve_targets(keys, values, beta_wide, growth):
    return jnp.concatenate(
        [beta_wide * growth * keys, widened(beta_wide, DV) * values], axis=1
    )


def head_terms(keys, values, beta_wide, log_wide):
    growth, tail, within = decay_parts(log_wide)
    lower = lower_system(keys, beta_wide, within)
    inverse = unit_inverse(lower)
    both = raw_dot(inverse, solve_targets(keys, values, beta_wide, growth), 1, 0)
    solved_keys = both[:, :DK]
    at, source = position_pair(DK, DK + DV)
    state = jnp.where(at == source, 1.0, 0.0)
    offset_rows = jnp.where(
        lax.broadcasted_iota(jnp.int32, both.shape, 1) >= DK, both, 0.0
    )
    decayed_keys = keys * tail
    for group in range(keys.shape[0] // GROUP):
        pseudo = offset_rows - mm(solved_keys, state)
        state = widened(group_decay(log_wide, group), DK + DV) * state + mm_tn(
            in_group(decayed_keys, group), pseudo
        )
    return inverse, both, state


def head_outputs(queries, keys, log_wide, both, gate_pre, head_gain, state):
    growth, tail, within = decay_parts(log_wide)
    attend = within * mm_nt(queries, keys)
    decayed_keys = keys * tail
    solved_keys, solved_values = both[:, :DK], both[:, DK:]
    stacked = jnp.concatenate([queries, solved_keys], axis=0)
    rows = queries.shape[0]
    read = 0.0
    for group in range(rows // GROUP):
        now = mm(stacked, state)
        pseudo_now = solved_values - now[rows:]
        read = read + jnp.concatenate(
            [in_group(now[:rows], group), in_group(now[rows:], group)], axis=0
        )
        state = widened(group_decay(log_wide, group), DV) * state + mm_tn(
            in_group(decayed_keys, group), pseudo_now
        )
    output_rows = widened(growth, DV) * read[:rows] + mm(attend, solved_values - read[rows:])
    normed = (
        output_rows
        * lax.rsqrt(jnp.mean(output_rows * output_rows, axis=-1, keepdims=True) + eps_norm)
        * head_gain
    )
    return normed * (gate_pre * jax.nn.sigmoid(gate_pre)), state


def head_whole(inverse, state, queries, keys, values, beta_wide, log_wide, gate_pre, head_gain):
    growth, _, within = decay_parts(log_wide)
    lower = lower_system(keys, beta_wide, within)
    both = solved(lower, solve_targets(keys, values, beta_wide, growth), inverse)
    return head_outputs(queries, keys, log_wide, both, gate_pre, head_gain, state)


def unit_rows_scaled(values, factor):
    return values * lax.rsqrt(jnp.sum(values * values, axis=-1, keepdims=True) + eps_unit) * factor


def rate_columns(rates, head):
    lane = lax.broadcasted_iota(jnp.int32, rates.shape, 1)
    beta = jnp.sum(jnp.where(lane == head, rates, 0.0), axis=1, keepdims=True)
    log_decay = jnp.sum(jnp.where(lane == head + H, rates, 0.0), axis=1, keepdims=True)
    wide = (rates.shape[0], DK)
    return jnp.broadcast_to(beta, wide), jnp.broadcast_to(log_decay, wide)


def head_inputs(query_conv, key_conv, rates, head):
    queries = unit_rows_scaled(query_conv, DK ** (-0.5))
    keys = unit_rows_scaled(key_conv, 1.0)
    beta_wide, log_wide = rate_columns(rates, head)
    return queries, keys, beta_wide, log_wide


def terms_kernel(query_ref, key_ref, value_ref, rates_ref, inverse_ref, both_ref, map_ref):
    _, keys, beta_wide, log_wide = head_inputs(
        query_ref[...], key_ref[...], rates_ref[...], pl.program_id(0)
    )
    inverse, both, state = head_terms(keys, value_ref[...], beta_wide, log_wide)
    inverse_ref[...] = inverse
    both_ref[...] = both
    map_ref[0] = state


def outputs_kernel(
    query_ref, key_ref, rates_ref, both_ref, gate_ref, gain_ref, state_ref, mixed_ref
):
    queries, keys, _, log_wide = head_inputs(
        query_ref[...], key_ref[...], rates_ref[...], pl.program_id(0)
    )
    mixed, _ = head_outputs(
        queries, keys, log_wide, both_ref[...], gate_ref[...], gain_ref[...], state_ref[0]
    )
    mixed_ref[...] = mixed.astype(mixed_ref.dtype)


def state_kernel(
    query_ref, key_ref, rates_ref, both_ref, gate_ref, gain_ref, state_ref, grad_ref, out_ref
):
    queries, keys, _, log_wide = head_inputs(
        query_ref[...], key_ref[...], rates_ref[...], pl.program_id(0)
    )

    def from_state(state):
        return head_outputs(
            queries, keys, log_wide, both_ref[...], gate_ref[...], gain_ref[...], state
        )[0]

    _, back = jax.vjp(from_state, state_ref[0])
    out_ref[0] = back(grad_ref[...])[0]


def backward_kernel(
    inverse_ref,
    state_ref,
    query_ref,
    key_ref,
    value_ref,
    rates_ref,
    gate_ref,
    gain_ref,
    grad_ref,
    state_grad_ref,
    query_out,
    key_out,
    value_out,
    rates_out,
    gate_out,
    gain_out,
):
    inverse, state = inverse_ref[...], state_ref[0]
    head = pl.program_id(0)

    def whole(query_conv, key_conv, values, rates, gate_pre, gain):
        queries, keys, beta_wide, log_wide = head_inputs(query_conv, key_conv, rates, head)
        return head_whole(
            inverse, state, queries, keys, values, beta_wide, log_wide, gate_pre, gain
        )

    _, back = jax.vjp(
        whole,
        query_ref[...],
        key_ref[...],
        value_ref[...],
        rates_ref[...],
        gate_ref[...],
        gain_ref[...],
    )
    grads = back((grad_ref[...], state_grad_ref[0]))
    query_out[...] = grads[0]
    key_out[...] = grads[1]
    value_out[...] = grads[2]
    gate_out[...] = grads[4].astype(gate_out.dtype)
    gain_out[0] = grads[5]

    @pl.when(head == 0)
    def first_head():
        rates_out[...] = grads[3]

    @pl.when(head > 0)
    def later_head():
        rates_out[...] = rates_out[...] + grads[3]


def columns_of(rows, width, first=0):
    return pl.BlockSpec((rows, width), lambda head: (0, head + first))


def matrix_of(rows, width):
    return pl.BlockSpec((1, rows, width), lambda head: (head, 0, 0))


def fixed_block(rows, width):
    return pl.BlockSpec((rows, width), lambda head: (0, 0))


def per_head(kernel, in_specs, out_specs, out_shapes):
    return pl.pallas_call(
        kernel, grid=(H,), in_specs=in_specs, out_specs=out_specs, out_shape=out_shapes
    )


def shape_of(*dims, kind=jnp.float32):
    return jax.ShapeDtypeStruct(dims, kind)


def run_terms(conv_out, rates):
    rows = conv_out.shape[0]
    return per_head(
        terms_kernel,
        [
            columns_of(rows, DK),
            columns_of(rows, DK, H),
            columns_of(rows, DV, 2 * KD // DV),
            fixed_block(rows, 2 * H),
        ],
        [columns_of(rows, rows), columns_of(rows, DK + DV), matrix_of(DK, DK + DV)],
        [
            shape_of(rows, H * rows),
            shape_of(rows, H * (DK + DV)),
            shape_of(H, DK, DK + DV),
        ],
    )(conv_out, conv_out, conv_out, rates)


def output_specs(rows):
    return [
        columns_of(rows, DK),
        columns_of(rows, DK, H),
        fixed_block(rows, 2 * H),
        columns_of(rows, DK + DV),
        columns_of(rows, DV, QKV // DV),
        fixed_block(1, DV),
        matrix_of(DK, DV),
    ]


def run_outputs(conv_out, rates, both, projected, gain_row, state):
    rows = conv_out.shape[0]
    return per_head(
        outputs_kernel,
        output_specs(rows),
        columns_of(rows, DV),
        shape_of(rows, H * DV, kind=jnp.bfloat16),
    )(conv_out, conv_out, rates, both, projected, gain_row, state)


def run_state(conv_out, rates, both, projected, gain_row, state, grad):
    rows = conv_out.shape[0]
    return per_head(
        state_kernel,
        output_specs(rows) + [columns_of(rows, DV)],
        matrix_of(DK, DV),
        shape_of(H, DK, DV),
    )(conv_out, conv_out, rates, both, projected, gain_row, state, grad)


def run_backward(inverse, state, conv_out, rates, projected, gain_row, grad, state_grad):
    rows = conv_out.shape[0]
    narrow, wide = columns_of(rows, DK), columns_of(rows, DV)
    return per_head(
        backward_kernel,
        [
            columns_of(rows, rows),
            matrix_of(DK, DV),
            narrow,
            columns_of(rows, DK, H),
            columns_of(rows, DV, 2 * KD // DV),
            fixed_block(rows, 2 * H),
            columns_of(rows, DV, QKV // DV),
            fixed_block(1, DV),
            wide,
            matrix_of(DK, DV),
        ],
        [narrow, narrow, wide, fixed_block(rows, 2 * H), wide, matrix_of(1, DV)],
        [
            shape_of(rows, H * DK),
            shape_of(rows, H * DK),
            shape_of(rows, H * DV),
            shape_of(rows, 2 * H),
            shape_of(rows, H * DV, kind=jnp.bfloat16),
            shape_of(H, 1, DV),
        ],
    )(
        inverse,
        state,
        conv_out,
        conv_out,
        conv_out,
        rates,
        projected,
        gain_row,
        grad,
        state_grad,
    )


def rate_parts(route_pre, decay_log, decay_bias):
    betas = jax.nn.sigmoid(route_pre[:, :H])
    log_decay = -jnp.exp(decay_log) * jax.nn.softplus(route_pre[:, H:] + decay_bias)
    return jnp.concatenate([betas, log_decay], axis=1)


def map_times(left, right):
    return jnp.einsum("hij,hjv->hiv", left, right, precision=highest_precision)


def sent_low(value, steps):
    return passed_along(value.astype(jnp.bfloat16), CTX_AXES, steps).astype(jnp.float32)


def window_maps(trans, direction):
    count = lax.axis_size(CTX_AXES)
    levels = [trans]
    window = 1
    while 2 * window < count:
        levels.append(map_times(levels[-1], sent_low(levels[-1], direction * window)))
        window = 2 * window
    return levels, sent_low(levels[-1], direction)


def carried_state(levels, near_trans, offset, direction):
    window = 1
    for trans in levels[:-1]:
        before = sent_low(offset, direction * window)
        offset = offset + map_times(trans, before)
        window = 2 * window
    near = sent_low(offset, direction)
    far = sent_low(offset, direction * (window + 1))
    return near + map_times(near_trans, far)


def swap_columns(rows, count):
    split = rows.reshape(rows.shape[0], count, rows.shape[1] // count)
    return jnp.transpose(split, (1, 0, 2))


def gathered_near(rows):
    chips = lax.axis_size(CHIP_AXES)
    own = lax.all_to_all(
        jnp.broadcast_to(rows[None], (chips,) + rows.shape),
        CHIP_AXES,
        split_axis=0,
        concat_axis=0,
        tiled=True,
    )
    own = own.reshape(-1, rows.shape[1])
    other = lax.ppermute(own, "core", [(0, 1), (1, 0)])
    first = lax.axis_index("core") == 0
    return jnp.concatenate([jnp.where(first, own, other), jnp.where(first, other, own)], axis=0)


def summed_rows(terms, columns):
    y_count, core_count, far_count, x_count = (lax.axis_size(axis) for axis in ALL_AXES)
    near_count = lax.axis_size(NEAR_AXES)
    rows = D // far_count
    split = terms.reshape(
        y_count, core_count, far_count, x_count, rows // near_count, columns
    )
    split = jnp.transpose(split, (2, 1, 0, 3, 4, 5)).reshape(far_count, rows, columns)
    mine = lax.axis_index("z")
    total = lax.dynamic_index_in_dim(split, mine, 0, keepdims=False).astype(jnp.float32)
    for step in range(1, far_count):
        pairs = [(source, (source + step) % far_count) for source in range(far_count)]
        leaving = lax.dynamic_index_in_dim(split, (mine + step) % far_count, 0, keepdims=False)
        arrived = lax.ppermute(leaving, "z", pairs)
        total = total + arrived.astype(jnp.float32)
    block = total.astype(jnp.bfloat16)
    return lax.all_to_all(
        block.reshape(near_count, rows // near_count, columns),
        NEAR_AXES,
        split_axis=0,
        concat_axis=0,
        tiled=True,
    )


def joined_columns(blocks):
    count, rows, columns = blocks.shape
    return jnp.transpose(blocks, (1, 0, 2)).reshape(rows, count * columns).astype(jnp.float32)


def summed_everywhere(vector):
    count = lax.axis_size(ALL_AXES)
    chunk = -(-vector.shape[0] // (count * 128)) * 128
    padded = jnp.pad(vector, (0, count * chunk - vector.shape[0])).reshape(count, chunk)
    parts = lax.all_to_all(padded, ALL_AXES, split_axis=0, concat_axis=0, tiled=True)
    total = jnp.broadcast_to(jnp.sum(parts, axis=0)[None], (count, chunk))
    whole = lax.all_to_all(total, ALL_AXES, split_axis=0, concat_axis=0, tiled=True)
    return whole.reshape(-1)[: vector.shape[0]]


def square_times(left, right):
    return jnp.dot(left, right, preferred_element_type=jnp.float32)


def orthogonal_rows(raw_rows):
    low = jnp.bfloat16
    raw = lax.all_gather(raw_rows, DP_AXES, axis=0, tiled=True)
    gram_raw = lax.optimization_barrier(times_transposed(raw, raw))
    norm = jnp.sqrt(jnp.trace(gram_raw))
    scale = 1.0 / (norm + eps_muon)
    gram = gram_raw * (scale * scale)
    factors = []
    for step in range(NS_STEPS):
        gram_low = gram.astype(low)
        factor = (poly_two * gram + poly_three * square_times(gram_low, gram_low)).astype(low)
        factors.append(factor)
        if step + 1 < NS_STEPS:
            turned = poly_one * gram + square_times(factor, gram_low)
            gram = poly_one * turned + square_times(turned.astype(low), factor)
    rows = raw_rows.shape[0]
    start = lax.axis_index(DP_AXES) * rows
    last = factors[-1]
    at = lax.broadcasted_iota(jnp.int32, (rows, D), 0) + start
    own = at == lax.broadcasted_iota(jnp.int32, (rows, D), 1)
    product = lax.dynamic_slice_in_dim(last, start, rows, axis=0).astype(jnp.float32)
    identity_part = poly_one
    for factor in factors[-2::-1]:
        product_low = product.astype(low)
        mine = lax.dynamic_slice_in_dim(factor, start, rows, axis=0).astype(jnp.float32)
        product = (
            poly_one * product + identity_part * mine + square_times(product_low, factor)
        )
        identity_part = identity_part * poly_one
    mapped = square_times(product.astype(low), raw)
    return ((identity_part * raw_rows.astype(jnp.float32) + mapped) * scale).astype(low)


def local(
    tokens_in,
    upstream,
    query_weight,
    key_weight,
    value_weight,
    gate_weight,
    output_weight,
    swiglu_gate,
    swiglu_up,
    swiglu_down,
    query_moment,
    key_moment,
    value_moment,
    gate_moment,
    output_moment,
    swiglu_gate_moment,
    swiglu_up_moment,
    swiglu_down_moment,
    small_params,
    small_moment,
):
    weights_in = (
        query_weight,
        key_weight,
        value_weight,
        gate_weight,
        output_weight,
        swiglu_gate,
        swiglu_up,
        swiglu_down,
    )
    moments_in = (
        query_moment,
        key_moment,
        value_moment,
        gate_moment,
        output_moment,
        swiglu_gate_moment,
        swiglu_up_moment,
        swiglu_down_moment,
    )
    low = jnp.bfloat16
    ctx_count = lax.axis_size(CTX_AXES)
    near_count = lax.axis_size(NEAR_AXES)
    gain_one, gain_two, head_gain, conv_taps, decay_log, decay_bias, route_weight = unpack_small(
        small_params
    )
    route_low = route_weight.astype(low)
    rim_rows = CONV - 1
    front_rows = jnp.concatenate([member.astype(low) for member in weights_in[:4]], axis=1)
    back_rows = jnp.concatenate([member.astype(low) for member in weights_in[4:]], axis=1)
    front_full = lax.all_gather(front_rows, ALL_AXES, axis=0, tiled=True)
    front_full, back_rows = lax.optimization_barrier((front_full, back_rows))
    back_full = lax.all_gather(back_rows, ALL_AXES, axis=0, tiled=True)
    output_full = back_full[:, :VD]
    gate_up_full = back_full[:, VD : VD + 2 * FF]
    down_full = back_full[:, VD + 2 * FF :]

    inputs_full = tokens_in[0].astype(jnp.float32)
    normed_one, norm_one_back = jax.vjp(root_norm, inputs_full, gain_one)
    normed_one_low = normed_one.astype(low)
    upstream_full = upstream[0]
    upstream_low = upstream_full.astype(low)
    early_left = gathered_near(jnp.concatenate([normed_one_low, upstream_low], axis=1))
    rim_pad = 16 - rim_rows
    prior_normed = passed_along(normed_one_low[normed_one_low.shape[0] - rim_rows :], CTX_AXES, 1)
    rim_left = gathered_near(jnp.pad(prior_normed, ((0, rim_pad), (0, 0))))
    front_left = jnp.concatenate(
        [
            early_left[:, :D].reshape(near_count, -1, D),
            rim_left.reshape(near_count, rim_rows + rim_pad, D),
        ],
        axis=1,
    ).reshape(-1, D)
    projected = matmul(normed_one_low, front_full)
    pre_proj = projected[:, :QKV]
    route_pre = matmul(normed_one_low, route_low)
    prior_rim = passed_along(
        pre_proj[pre_proj.shape[0] - rim_rows :].astype(low), CTX_AXES, 1
    ).astype(jnp.float32)
    extended = jnp.concatenate([prior_rim, pre_proj], axis=0)
    conv_out, conv_back = jax.vjp(conv_silu, extended, conv_taps)
    rates, rates_back = jax.vjp(rate_parts, route_pre, decay_log, decay_bias)
    gain_row = head_gain[None]

    inverse, both, maps = run_terms(conv_out, rates)
    trans, offset = maps[:, :, :DK], maps[:, :, DK:]
    levels, near_trans = window_maps(trans, 1)
    state_in = carried_state(levels, near_trans, offset, 1)
    back_levels, back_near = window_maps(jnp.swapaxes(trans, 1, 2), -1)
    mixed_low = run_outputs(conv_out, rates, both, projected, gain_row, state_in)
    residual_one = inputs_full + times_transposed(mixed_low, output_full)
    normed_two, norm_two_back = jax.vjp(root_norm, residual_one, gain_two)
    normed_two_low = normed_two.astype(low)
    gate_up = matmul(normed_two_low, gate_up_full)
    gate_act, up_act = gate_up[:, :FF], gate_up[:, FF:]
    sigma = jax.nn.sigmoid(gate_act)
    middle = (gate_act * sigma * up_act).astype(low)
    block_out = residual_one + times_transposed(middle, down_full)

    grad_middle = matmul(upstream_low, down_full)
    grad_gate = (grad_middle * up_act * sigma * (1.0 + gate_act * (1.0 - sigma))).astype(low)
    grad_up = (grad_middle * gate_act * sigma).astype(low)
    grad_gate_up = jnp.concatenate([grad_gate, grad_up], axis=1)
    grad_normed_two = times_transposed(grad_gate_up, gate_up_full)
    grad_residual_norm, grad_gain_two = norm_two_back(grad_normed_two)
    grad_residual = upstream_full + grad_residual_norm
    grad_residual_low = grad_residual.astype(low)
    grad_mixed = matmul(grad_residual_low, output_full)

    late_left = gathered_near(jnp.concatenate([normed_two_low, grad_residual_low], axis=1))
    back_columns = jnp.concatenate(
        [swap_columns(member, near_count) for member in (mixed_low, grad_gate_up, middle)], axis=2
    )
    back_columns = lax.all_to_all(back_columns, NEAR_AXES, split_axis=0, concat_axis=0, tiled=True)
    state_grad = run_state(conv_out, rates, both, projected, gain_row, state_in, grad_mixed)
    state_out_grad = carried_state(back_levels, back_near, state_grad, -1)

    (query_grad, key_grad, value_grad, rates_grad, grad_gate_pre_low, gain_grads) = run_backward(
        inverse, state_in, conv_out, rates, projected, gain_row, grad_mixed, state_out_grad
    )
    grad_conv = jnp.concatenate([query_grad, key_grad, value_grad], axis=1)
    grad_extended, grad_conv_taps = conv_back(grad_conv)
    grad_route_pre, grad_decay_log, grad_decay_bias = rates_back(rates_grad)
    grad_head_gain = jnp.sum(gain_grads, axis=(0, 1))
    back_rim = passed_along(shortened(grad_extended[:rim_rows]), CTX_AXES, -1)
    grad_pre = grad_extended[rim_rows:]
    split_row = grad_pre.shape[0] - rim_rows
    grad_pre = jnp.concatenate([grad_pre[:split_row], grad_pre[split_row:] + back_rim], axis=0)
    grad_front_low = jnp.concatenate([grad_pre.astype(low), grad_gate_pre_low], axis=1)
    grad_route_low = grad_route_pre.astype(low)
    front_parts = jnp.concatenate(
        [
            jnp.concatenate(
                [
                    grad_extended[rim_rows:],
                    grad_extended[:rim_rows],
                    jnp.zeros((rim_pad, QKV), jnp.float32),
                ],
                axis=0,
            ).astype(low),
            jnp.pad(grad_gate_pre_low, ((0, rim_rows + rim_pad), (0, 0))),
        ],
        axis=1,
    )

    front_columns = lax.all_to_all(
        swap_columns(front_parts, near_count),
        NEAR_AXES,
        split_axis=0,
        concat_axis=0,
        tiled=True,
    )
    count_rows = near_count * grad_front_low.shape[0]
    widths = (VD // near_count, 2 * FF // near_count, FF // near_count)
    back_columns = back_columns.reshape(count_rows, sum(widths))
    piece_out = back_columns[:, : widths[0]]
    piece_gate_up = back_columns[:, widths[0] : widths[0] + widths[1]]
    piece_down = back_columns[:, widths[0] + widths[1] :]
    back_terms = jnp.concatenate(
        [
            transposed_times(late_left[:, D:], piece_out).astype(low),
            transposed_times(late_left[:, :D], piece_gate_up).astype(low),
            transposed_times(early_left[:, D:], piece_down).astype(low),
        ],
        axis=1,
    )
    back_blocks = summed_rows(back_terms, sum(widths))
    front_width = grad_front_low.shape[1] // near_count
    front_terms = transposed_times(
        front_left, front_columns.reshape(front_left.shape[0], front_width)
    ).astype(low)
    front_blocks = summed_rows(front_terms, front_width)
    front_grads = joined_columns(front_blocks)
    gate_up_grads = joined_columns(back_blocks[:, :, widths[0] : widths[0] + widths[1]])
    gradients = (
        front_grads[:, :KD],
        front_grads[:, KD : 2 * KD],
        front_grads[:, 2 * KD : QKV],
        front_grads[:, QKV:],
        joined_columns(back_blocks[:, :, : widths[0]]),
        gate_up_grads[:, :FF],
        gate_up_grads[:, FF:],
        joined_columns(back_blocks[:, :, widths[0] + widths[1] :]),
    )

    route_weight_grad = transposed_times(normed_one_low, grad_route_low)
    grad_normed_one = times_transposed(grad_front_low, front_full) + times_transposed(
        grad_route_low, route_low
    )
    grad_inputs, grad_gain_one = norm_one_back(grad_normed_one)
    input_grad = grad_residual + grad_inputs
    small_local = pack_small(
        (
            grad_gain_one,
            grad_gain_two,
            grad_head_gain,
            grad_conv_taps,
            grad_decay_log,
            grad_decay_bias,
            route_weight_grad,
        )
    )
    moments_new = tuple(
        (moment_rate * moment + gradient for moment, gradient in zip(moments_in, gradients))
    )
    squares_local = jnp.stack([jnp.sum(member * member) for member in moments_new])

    repeats = ctx_count // 8
    outgoing = jnp.stack(
        [
            jnp.pad(moments_new[owner // repeats].astype(low), ((0, 0), (0, FF - moments_new[owner // repeats].shape[1])))
            for owner in range(ctx_count)
        ]
    )
    received = lax.all_to_all(outgoing, CTX_AXES, split_axis=0, concat_axis=0, tiled=True)
    ortho = orthogonal_rows(received.reshape(-1, FF))
    returned = lax.all_to_all(
        ortho.reshape(received.shape), CTX_AXES, split_axis=0, concat_axis=0, tiled=True
    )
    weights_new = []
    for index in range(8):
        columns_now = weights_in[index].shape[1]
        factor = matrix_rate * math.sqrt(max(1.0, columns_now / D))
        weights_new.append(
            weights_in[index]
            - factor * returned[index * repeats, :, :columns_now].astype(jnp.float32)
        )
    summed = summed_everywhere(jnp.concatenate([small_local, squares_local]))
    small_grad = summed[: small_local.shape[0]]
    moment_norms = jnp.sqrt(summed[small_local.shape[0] :])
    small_moment_new = moment_rate * small_moment + small_grad
    small_new = small_params - small_rate * small_moment_new
    return (
        block_out[None],
        input_grad[None],
        *gradients,
        *weights_new,
        *moments_new,
        small_grad,
        small_new,
        small_moment_new,
        moment_norms,
    )


def solution(mesh):
    dp_count, ctx_count = mesh.shape["dp"], mesh.shape["ctx"]
    split_mesh = Mesh(mesh.devices.reshape(dp_count // 2, 2, ctx_count // 2, 2), ALL_AXES)
    tokens, rows, copied = P(DP_AXES, CTX_AXES, None), P(ALL_AXES, None), P()
    in_specs = (tokens,) * 2 + (rows,) * 16 + (copied,) * 2
    out_specs = (tokens,) * 2 + (rows,) * 24 + (copied,) * 4

    return jax.shard_map(
        local, mesh=split_mesh, in_specs=in_specs, out_specs=out_specs, check_vma=False
    )
```
